256 devices in a mesh: tm: 8 (over z), height: 16 (over x, y), width: 2 (over core).
Axes of the slice: x: 4, y: 4, z: 8, core: 2. Of those that a mesh axis runs over, the one named last changes fastest.
Arguments:
- video: bfloat16 [2, 128, 16, 256, 128], P('width', ('tm', 'height')), may hold values from -6 to 6
- out_grad: bfloat16 [2, 128, 16, 256, 128], P('width', None, 'tm', 'height'), may hold values from -6 to 6
- lengths: int32 [4], replicated, may hold values from 1 to 6, 16 in all
- temporal_weight: bfloat16 [3, 128, 128], replicated, may hold values from -0.3125 to 0.3125
- spatial_weight: bfloat16 [3, 3, 128, 128], replicated, may hold values from -0.1875 to 0.1875
Outputs:
- video_grad: bfloat16 [2, 128, 16, 256, 128], P('width', ('tm', 'height'))
- temporal_grad: float32 [3, 128, 128], replicated
- spatial_grad: float32 [3, 3, 128, 128], replicated
The draws below stay inside these ranges and needn't reach their ends.
Inputs may be any that keep to these rules, and one draw needn't show every extreme that they name: The 4 clips lie end to end in frame order, their lengths sum to 16, and the longest clip has exactly 6 frames.
All inputs are finite; a program needn't handle non-finite values.
Results may differ from the reference program's by a relative error of at most 0.008.
Values may be sent and summed in bfloat16 or wider, within the bound.
A program may use at most 128 MiB of HBM per device.

```python
import math
import jax
import jax.numpy as jnp
import numpy as np
from jax import lax

C = 128
NCLIP = 4
H = 256
F = 16
WL = 128
N_WIDTH = 2


def steps_of(stream_key, extent, split, smallest, largest):
    factor_of = 1.0
    for dim, parts in split:
        steps = jax.random.uniform(jax.random.fold_in(jax.random.fold_in(stream_key, 6), dim), (parts,), jnp.float32, smallest / len(split), largest / len(split))
        factor_of = factor_of * jnp.repeat(jnp.exp(steps), extent[dim] // parts).reshape((-1,) + (1,) * (len(extent) - 1 - dim))
    return factor_of


def length_profile(number_of, total, most, skew):
    loads = [(1 << 20) // math.isqrt(standing ** skew) + 1 for standing in range(2, number_of + 1)]
    rest, counts = total - most - (number_of - 1), [1] * (number_of - 1)
    while rest > 0:
        movable = [i for i in range(number_of - 1) if counts[i] < most]
        mass, budget = sum([loads[i] for i in movable]), rest
        for i in movable:
            extra = min(most - counts[i], max(1, budget * loads[i] // mass), rest)
            counts[i] = counts[i] + extra
            rest = rest - extra
    return np.array([most] + counts)


def ragged(key, number_of, total, reach, lean):
    if number_of == 2:
        one = jax.random.randint(key, (), max(1, total - reach), min(reach, total - 1) + 1)
        return jnp.stack([one, total - one])
    sizes = jnp.asarray(length_profile(number_of, total, reach, lean), jnp.int32)
    couples = (number_of - 1) // 2
    donor, sink = sizes[1:1 + 2 * couples:2], sizes[2:2 + 2 * couples:2]
    room = jnp.minimum(donor - 1, reach - sink)
    shifted = jax.random.randint(jax.random.fold_in(key, 1), (couples,), 0, 1 << 20) % (room + 1)
    sizes = sizes.at[1:1 + 2 * couples:2].set(donor - shifted).at[2:2 + 2 * couples:2].set(sink + shifted)
    return sizes[jax.random.permutation(jax.random.fold_in(key, 2), number_of)]


def centred(own_key, dims, width, most, cuts=(), kind=jnp.bfloat16):
    array = jax.random.normal(own_key, dims, jnp.float32) * width
    if len(cuts) > 0:
        array = steps_of(own_key, dims, cuts, -0.22, 0.18) * array
    return jnp.clip(array, min=-most, max=most).astype(kind)


def setup_inputs(seed: int = 0) -> dict:
    key_of = jax.random.split(jax.random.key(seed), 6)
    return {
        "video": centred(key_of[0], (N_WIDTH, WL, F, H, C), 1.0, 6.0, ((0, 2), (1, 128))),
        "out_grad": centred(key_of[1], (N_WIDTH, WL, F, H, C), 1.0, 6.0, ((0, 2), (2, 8), (3, 16))),
        "lengths": ragged(key_of[2], NCLIP, F, F // 3 + 1, 2).astype(jnp.int32),
        "temporal_weight": centred(key_of[3], (3, C, C), (3 * C) ** -0.5, 0.3125),
        "spatial_weight": centred(key_of[4], (3, 3, C, C), (9 * C) ** -0.5, 0.1875),
    }


def frame_masks(lengths, frames):
    ends = jnp.cumsum(lengths, dtype=jnp.int32)
    starts = ends - lengths
    frame_index = jnp.arange(frames, dtype=jnp.int32)
    inside = (frame_index[:, None] >= starts[None, :]) & (frame_index[:, None] < ends[None, :])
    first = jnp.sum(jnp.where(inside, starts[None, :], 0), axis=1, dtype=jnp.int32)
    return jnp.stack([(frame_index - lag >= first) for lag in range(3)]).astype(jnp.bfloat16)


def silu_slope(pre, grads):
    sig = jax.nn.sigmoid(pre)
    return grads.astype(jnp.float32) * sig * (1.0 + pre * (1.0 - sig))


def reference(video, out_grad, lengths, temporal_weight, spatial_weight):
    halves = video.shape[0]
    frames = video.shape[2]
    rows = video.shape[3]
    chans = video.shape[4]
    cols = halves * video.shape[1]
    clip = jnp.transpose(video, (2, 3, 0, 1, 4)).reshape(frames, rows, cols, chans)
    grads = jnp.transpose(out_grad, (2, 3, 0, 1, 4)).reshape(frames, rows, cols, chans)
    masks = frame_masks(lengths, frames)
    padded = jnp.pad(clip, ((2, 0), (0, 0), (0, 0), (0, 0)))
    frame_ids = jnp.arange(frames, dtype=jnp.int32)

    def tap(frame, lag):
        piece = lax.dynamic_index_in_dim(padded, frame + 2 - lag, 0, keepdims=False)
        weight = lax.dynamic_index_in_dim(masks[lag], frame, 0, keepdims=False)
        return (piece * weight).reshape(-1, chans)

    def forward_frame(frame):
        total = jnp.zeros((rows * cols, chans), jnp.float32)
        for lag in range(3):
            total = total + jnp.dot(tap(frame, lag), temporal_weight[lag], preferred_element_type=jnp.float32)
        return total.astype(jnp.bfloat16).reshape(rows, cols, chans)

    act = lax.map(forward_frame, frame_ids)

    def spatial_step(accum, inputs):
        act_frame, grad_frame = inputs
        padded_act = jnp.pad(act_frame, ((1, 1), (1, 1), (0, 0)))
        pre = jnp.zeros((rows * cols, chans), jnp.float32)
        for row_off in range(3):
            for col_off in range(3):
                piece = padded_act[row_off:row_off + rows, col_off:col_off + cols].reshape(-1, chans)
                pre = pre + jnp.dot(piece, spatial_weight[row_off, col_off], preferred_element_type=jnp.float32)
        delta = silu_slope(pre, grad_frame.reshape(-1, chans)).astype(jnp.bfloat16)
        padded_delta = jnp.pad(delta.reshape(rows, cols, chans), ((1, 1), (1, 1), (0, 0)))
        back = jnp.zeros((rows * cols, chans), jnp.float32)
        terms = []
        for row_off in range(3):
            line = []
            for col_off in range(3):
                piece = padded_delta[2 - row_off:2 - row_off + rows, 2 - col_off:2 - col_off + cols].reshape(-1, chans)
                back = back + jnp.dot(piece, spatial_weight[row_off, col_off].T, preferred_element_type=jnp.float32)
                source = padded_act[row_off:row_off + rows, col_off:col_off + cols].reshape(-1, chans)
                line.append(lax.dot_general(source, delta, (((0,), (0,)), ((), ())), preferred_element_type=jnp.float32))
            terms.append(jnp.stack(line))
        return accum + jnp.stack(terms), back.astype(jnp.bfloat16).reshape(rows, cols, chans)

    spatial_sum, act_grad = lax.scan(spatial_step, jnp.zeros((3, 3, chans, chans), jnp.float32), (act, grads))
    padded_grad = jnp.pad(act_grad, ((0, 2), (0, 0), (0, 0), (0, 0)))
    padded_mask = jnp.pad(masks, ((0, 0), (0, 2)))

    def backward_step(accum, frame):
        total = jnp.zeros((rows * cols, chans), jnp.float32)
        current = lax.dynamic_index_in_dim(act_grad, frame, 0, keepdims=False).reshape(-1, chans)
        terms = []
        for lag in range(3):
            later = lax.dynamic_index_in_dim(padded_grad, frame + lag, 0, keepdims=False)
            weight = lax.dynamic_index_in_dim(padded_mask[lag], frame + lag, 0, keepdims=False)
            total = total + jnp.dot((later * weight).reshape(-1, chans), temporal_weight[lag].T, preferred_element_type=jnp.float32)
            terms.append(lax.dot_general(tap(frame, lag), current, (((0,), (0,)), ((), ())), preferred_element_type=jnp.float32))
        return accum + jnp.stack(terms), total.astype(jnp.bfloat16).reshape(rows, cols, chans)

    temporal_sum, frame_grad = lax.scan(backward_step, jnp.zeros((3, chans, chans), jnp.float32), frame_ids)
    video_grad = jnp.transpose(frame_grad.reshape(frames, rows, halves, cols // halves, chans), (2, 3, 0, 1, 4))
    scale = float(frames * rows * cols) ** -0.5
    return video_grad, temporal_sum * scale, spatial_sum * scale
```

```python
import functools

import jax
import jax.numpy as jnp
from jax import lax
from jax.experimental import pallas as pl
from jax.experimental.pallas import tpu as pltpu
from jax.sharding import PartitionSpec as P

MESH = pl.DeviceIdType.MESH


def reduce_kernel(n_tm, n_h, x_ref, o_ref, pair_buf, half, h_buf, z_buf, pair_sem, h_send, h_recv, z_send, z_recv, g_send, g_recv, f_send, f_recv):
    tm = lax.axis_index("tm")
    h = lax.axis_index("height")
    w = lax.axis_index("width")
    rows = x_ref.shape[0]
    half_rows = rows // 2
    piece = half_rows // n_h
    barrier = pltpu.get_barrier_semaphore()
    pl.semaphore_signal(barrier, inc=1, device_id=(tm, h, 1 - w), device_id_type=MESH)

    def greet_h(d, _):
        pl.semaphore_signal(barrier, inc=1, device_id=(tm, (h + d) % n_h, w), device_id_type=MESH)
        return _

    def greet_z(d, _):
        pl.semaphore_signal(barrier, inc=1, device_id=((tm + d) % n_tm, h, w), device_id_type=MESH)
        return _

    lax.fori_loop(1, n_h, greet_h, 0)
    lax.fori_loop(1, n_tm, greet_z, 0)
    pl.semaphore_wait(barrier, 1 + n_h - 1 + n_tm - 1)

    other = pl.multiple_of((1 - w) * half_rows, half_rows)
    mine = pl.multiple_of(w * half_rows, half_rows)
    pair = pltpu.make_async_remote_copy(
        src_ref=x_ref.at[pl.ds(other, half_rows)], dst_ref=pair_buf, send_sem=pair_sem.at[0], recv_sem=pair_sem.at[1],
        device_id=(tm, h, 1 - w), device_id_type=MESH)
    pair.start()
    pair.wait()
    half[...] = x_ref[pl.ds(mine, half_rows), :] + pair_buf[...]

    def h_copy(d):
        to = (h + d) % n_h
        return pltpu.make_async_remote_copy(
            src_ref=half.at[pl.ds(pl.multiple_of(to * piece, 8), piece)], dst_ref=h_buf.at[d],
            send_sem=h_send.at[d], recv_sem=h_recv.at[d], device_id=(tm, to, w), device_id_type=MESH)

    def go(copy):
        def body(d, _):
            copy(d).start()
            return _
        return body

    def done(copy):
        def body(d, _):
            copy(d).wait()
            return _
        return body

    lax.fori_loop(1, n_h, go(h_copy), 0)
    lax.fori_loop(1, n_h, done(h_copy), 0)
    h_buf[0] = half[pl.ds(pl.multiple_of(h * piece, 8), piece), :]
    total = h_buf[0]
    for d in range(1, n_h):
        total = total + h_buf[d]
    z_buf[tm] = total

    def z_copy(d):
        to = (tm + d) % n_tm
        return pltpu.make_async_remote_copy(
            src_ref=z_buf.at[tm], dst_ref=z_buf.at[tm],
            send_sem=z_send.at[d], recv_sem=z_recv.at[d], device_id=(to, h, w), device_id_type=MESH)

    lax.fori_loop(1, n_tm, go(z_copy), 0)
    lax.fori_loop(1, n_tm, done(z_copy), 0)
    total = z_buf[0]
    for t in range(1, n_tm):
        total = total + z_buf[t]
    here = pl.ds(pl.multiple_of(mine + h * piece, 8), piece)
    o_ref[here, :] = total

    def g_copy(d):
        to = (h + d) % n_h
        return pltpu.make_async_remote_copy(
            src_ref=o_ref.at[here], dst_ref=o_ref.at[here],
            send_sem=g_send.at[d], recv_sem=g_recv.at[d], device_id=(tm, to, w), device_id_type=MESH)

    def f_copy(d):
        owner = (h + n_h - d) % n_h
        there = pl.ds(pl.multiple_of(mine + owner * piece, 8), piece)
        return pltpu.make_async_remote_copy(
            src_ref=o_ref.at[there], dst_ref=o_ref.at[there],
            send_sem=f_send.at[d], recv_sem=f_recv.at[d], device_id=(tm, h, 1 - w), device_id_type=MESH)

    lax.fori_loop(1, n_h, go(g_copy), 0)
    f_copy(0).start()

    def forward(d, _):
        g_copy(d).wait()
        f_copy(d).start()
        return _

    lax.fori_loop(1, n_h, forward, 0)
    lax.fori_loop(0, n_h, done(f_copy), 0)


def all_reduce(x, n_tm, n_h):
    rows, lanes = x.shape
    half_rows = rows // 2
    piece = half_rows // n_h
    dma = pltpu.SemaphoreType.DMA
    return pl.pallas_call(
        functools.partial(reduce_kernel, n_tm, n_h),
        out_shape=jax.ShapeDtypeStruct((rows, lanes), jnp.float32),
        in_specs=[pl.BlockSpec(memory_space=pltpu.VMEM)],
        out_specs=pl.BlockSpec(memory_space=pltpu.VMEM),
        scratch_shapes=[
            pltpu.VMEM((half_rows, lanes), jnp.float32),
            pltpu.VMEM((half_rows, lanes), jnp.float32),
            pltpu.VMEM((n_h, piece, lanes), jnp.float32),
            pltpu.VMEM((n_tm, piece, lanes), jnp.float32),
            dma((2,)), dma((n_h,)), dma((n_h,)), dma((n_tm,)), dma((n_tm,)), dma((n_h,)), dma((n_h,)), dma((n_h,)), dma((n_h,)),
        ],
        compiler_params=pltpu.CompilerParams(collective_id=0, has_side_effects=True),
    )(x)


def with_halo(cells, n_tm, n_w):
    def joined(cells, axis, order, dim):
        head = lax.slice_in_dim(cells, 0, 1, axis=dim)
        tail = lax.slice_in_dim(cells, cells.shape[dim] - 1, cells.shape[dim], axis=dim)
        before = lax.ppermute(tail, axis, list(zip(order[:-1], order[1:])))
        after = lax.ppermute(head, axis, list(zip(order[1:], order[:-1])))
        return jnp.concatenate([before, cells, after], axis=dim)

    cells = joined(cells, "height", list(range(lax.axis_size("height"))), 2)
    return joined(cells, ("tm", "width"), [t * n_w + w for w in range(n_w) for t in range(n_tm)], 0)


def frame_masks(lengths, frames):
    ends = jnp.cumsum(lengths, dtype=jnp.int32)
    starts = ends - lengths
    frame_index = jnp.arange(frames, dtype=jnp.int32)
    inside = (frame_index[:, None] >= starts[None, :]) & (frame_index[:, None] < ends[None, :])
    first = jnp.sum(jnp.where(inside, starts[None, :], 0), axis=1, dtype=jnp.int32)
    return jnp.stack([frame_index - lag >= first for lag in range(3)]).astype(jnp.bfloat16)


def silu_slope(pre, grads):
    sig = jax.nn.sigmoid(pre)
    return grads.astype(jnp.float32) * sig * (1.0 + pre * (1.0 - sig))


def flatten(block):
    return block.reshape(-1, block.shape[-1])


def shards(video, out_grad, lengths, temporal_weight, spatial_weight):
    frames = video.shape[2]
    rows = video.shape[3]
    chans = video.shape[4]
    n_tm = lax.axis_size("tm")
    n_height = lax.axis_size("height")
    frames_dev = frames // n_tm
    rows_dev = rows // n_height
    cols_half = out_grad.shape[1]
    cols_dev = cols_half // n_tm
    total_cols = cols_half * lax.axis_size("width")
    masks = frame_masks(lengths, frames)
    bands = video[0, 0].reshape(frames, n_height, rows_dev, chans).transpose(1, 0, 2, 3)
    tile = lax.all_to_all(bands, "height", split_axis=0, concat_axis=0, tiled=True)
    grads = lax.all_to_all(out_grad[0], "tm", split_axis=0, concat_axis=0, tiled=True)
    grads = grads.reshape(n_tm, cols_dev, frames_dev, rows_dev, chans).transpose(1, 0, 2, 3, 4).reshape(cols_dev, frames, rows_dev, chans)
    padded = jnp.pad(tile, ((0, 0), (2, 0), (0, 0), (0, 0)))
    taps = [padded[:, 2 - lag : 2 - lag + frames] * masks[lag][None, :, None, None] for lag in range(3)]
    total = None
    for lag in range(3):
        term = jnp.dot(flatten(taps[lag]), temporal_weight[lag], preferred_element_type=jnp.float32)
        total = term if total is None else total + term
    act = total.astype(jnp.bfloat16).reshape(tile.shape)
    n_width = lax.axis_size("width")
    padded_act = with_halo(act, n_tm, n_width)
    pre = None
    for row_off in range(3):
        for col_off in range(3):
            piece = flatten(padded_act[col_off : col_off + cols_dev, :, row_off : row_off + rows_dev])
            term = jnp.dot(piece, spatial_weight[row_off, col_off], preferred_element_type=jnp.float32)
            pre = term if pre is None else pre + term
    delta = silu_slope(pre, flatten(grads)).astype(jnp.bfloat16).reshape(tile.shape)
    padded_delta = with_halo(delta, n_tm, n_width)
    flat_delta = flatten(delta)
    back = None
    spatial_terms = []
    for row_off in range(3):
        for col_off in range(3):
            piece = flatten(padded_delta[2 - col_off : 2 - col_off + cols_dev, :, 2 - row_off : 2 - row_off + rows_dev])
            term = jnp.dot(piece, spatial_weight[row_off, col_off].T, preferred_element_type=jnp.float32)
            back = term if back is None else back + term
            source = flatten(padded_act[col_off : col_off + cols_dev, :, row_off : row_off + rows_dev])
            spatial_terms.append(
                lax.dot_general(source, flat_delta, (((0,), (0,)), ((), ())), preferred_element_type=jnp.float32)
            )
    act_grad = back.astype(jnp.bfloat16).reshape(tile.shape)
    flat_grad = flatten(act_grad)
    frame_total = None
    temporal_terms = []
    for lag in range(3):
        temporal_terms.append(
            lax.dot_general(flatten(taps[lag]), flat_grad, (((0,), (0,)), ((), ())), preferred_element_type=jnp.float32)
        )
        masked = flatten(act_grad * masks[lag][None, :, None, None])
        product = jnp.dot(masked, temporal_weight[lag].T, preferred_element_type=jnp.float32).reshape(tile.shape)
        moved = jnp.pad(product[:, lag:], ((0, 0), (0, lag), (0, 0), (0, 0)))
        frame_total = moved if frame_total is None else frame_total + moved
    scale = float(frames * rows * total_cols) ** (-0.5)
    terms = jnp.concatenate(spatial_terms + temporal_terms, axis=0) * scale
    summed = all_reduce(terms, n_tm, n_height)
    moved = lax.all_to_all(frame_total.astype(jnp.bfloat16), "height", split_axis=0, concat_axis=0, tiled=True)
    video_grad = moved.transpose(1, 0, 2, 3).reshape(1, 1, frames, rows, chans)
    return (
        video_grad,
        summed[9 * chans :].reshape(3, chans, chans),
        summed[: 9 * chans].reshape(3, 3, chans, chans),
    )


def solution(mesh):
    placed = (
        P("width", ("tm", "height"), None, None, None),
        P("width", None, "tm", "height", None),
        P(),
        P(),
        P(),
    )
    return jax.shard_map(
        shards,
        mesh=mesh,
        in_specs=placed,
        out_specs=(P("width", ("tm", "height"), None, None, None), P(), P()),
        check_vma=False,
    )
```

```python
import functools

import jax
import jax.numpy as jnp
from jax import lax
from jax.experimental import pallas as pl
from jax.experimental.pallas import tpu as pltpu
from jax.sharding import PartitionSpec as P

MESH = pl.DeviceIdType.MESH
BF16 = jnp.bfloat16
F32 = jnp.float32


def started(copy):
    def body(d, carry):
        copy(d).start()
        return carry

    return body


def waited(copy):
    def body(d, carry):
        copy(d).wait()
        return carry

    return body


def kernel(
    n_tm, n_h, n_w, scale,
    video, out_grad, lengths, t_weight, s_weight,
    video_grad, sums,
    clip, grads, act, act_cols, act_rows, act_edge, delta, delta_cols, delta_rows, delta_edge,
    slope, act_grad, moved, plane, wide, s_total, terms, half, pair_buf, h_buf, z_buf,
    t_fwd, t_bwd, s_fwd, s_bwd,
    local_sem, vz_send, vz_recv, vh_send, vh_recv, a_send, a_recv, d_send, d_recv, o_send, o_recv,
    pair_sem, h_send, h_recv, z_send, z_recv, g_send, g_recv, f_send, f_recv,
):
    tm = lax.axis_index("tm")
    h = lax.axis_index("height")
    w = lax.axis_index("width")
    frames, cols, rows, chans = delta.shape
    pair = frames // n_tm
    up, down = (h + n_h - 1) % n_h, (h + 1) % n_h
    block = w * n_tm + tm
    blocks = n_w * n_tm
    left, right = (block + blocks - 1) % blocks, (block + 1) % blocks
    left_tm, left_w = left % n_tm, left // n_tm
    right_tm, right_w = right % n_tm, right // n_tm
    around = (
        (tm, up, w), (tm, down, w),
        (left_tm, h, left_w), (left_tm, up, left_w), (left_tm, down, left_w),
        (right_tm, h, right_w), (right_tm, up, right_w), (right_tm, down, right_w),
    )

    barrier = pltpu.get_barrier_semaphore()

    def greet_h(d, carry):
        pl.semaphore_signal(barrier, inc=1, device_id=(tm, (h + d) % n_h, w), device_id_type=MESH)
        return carry

    def greet_z(d, carry):
        pl.semaphore_signal(barrier, inc=1, device_id=((tm + d) % n_tm, h, w), device_id_type=MESH)
        return carry

    lax.fori_loop(1, n_tm, greet_z, 0)
    lax.fori_loop(1, n_h, greet_h, 0)
    pl.semaphore_signal(barrier, inc=1, device_id=(tm, h, 1 - w), device_id_type=MESH)
    for other in around[2:]:
        pl.semaphore_signal(barrier, inc=1, device_id=other, device_id_type=MESH)
    pl.semaphore_wait(barrier, n_tm - 1 + n_h - 1 + 1 + 6)

    def vz_copy(d):
        to = (tm + d) % n_tm
        return pltpu.make_async_remote_copy(
            src_ref=out_grad.at[0, pl.ds(to * cols, cols)], dst_ref=grads.at[tm],
            send_sem=vz_send.at[d], recv_sem=vz_recv.at[d], device_id=(to, h, w), device_id_type=MESH)

    def vh_copy(d):
        to = (h + d) % n_h
        return pltpu.make_async_remote_copy(
            src_ref=video.at[0, 0, :, pl.ds(pl.multiple_of(to * rows, rows), rows)], dst_ref=clip.at[pl.ds(2, frames), h],
            send_sem=vh_send.at[d], recv_sem=vh_recv.at[d], device_id=(tm, to, w), device_id_type=MESH)

    def step_of(j):
        return (((j + 1) // 2) * (2 * (j % 2) - 1) + n_tm) % n_tm

    lax.fori_loop(1, n_tm, lambda j, carry: started(vz_copy)(step_of(j), carry), 0)
    lax.fori_loop(1, n_h, started(vh_copy), 0)
    own_grad = pltpu.make_async_copy(out_grad.at[0, pl.ds(tm * cols, cols)], grads.at[tm], local_sem.at[0])
    own_clip = pltpu.make_async_copy(
        video.at[0, 0, :, pl.ds(pl.multiple_of(h * rows, rows), rows)], clip.at[pl.ds(2, frames), h], local_sem.at[1])
    own_grad.start()
    own_clip.start()

    for f in range(2):
        clip[f] = jnp.zeros((cols, rows, chans), BF16)
        act_grad[frames + f] = jnp.zeros((cols * rows, chans), BF16)
    for k in range(3):
        t_fwd[k * chans : (k + 1) * chans, :] = t_weight[k]
        t_bwd[k * chans : (k + 1) * chans, :] = t_weight[k].T
    for b in range(3):
        for a in range(3):
            place = pl.ds((b * 3 + a) * chans, chans)
            s_fwd[place, :] = s_weight[a, b]
            s_bwd[place, :] = s_weight[a, b].T
    s_total[...] = jnp.zeros_like(s_total)
    starts = [lengths[0], lengths[0] + lengths[1], lengths[0] + lengths[1] + lengths[2]]

    def mask(f, lag):
        keep = jnp.where(f >= lag, 1, 0)
        for start in starts:
            keep = jnp.where((start > f - lag) & (start <= f), 0, keep)
        return jnp.broadcast_to(keep.astype(F32), (rows, chans)).astype(BF16)[None]

    own_clip.wait()
    lax.fori_loop(1, n_h, waited(vh_copy), 0)

    def edges_of(value, edge, f):
        plane[...] = value.astype(F32)
        edge[0, f] = plane[pl.ds(0, cols, stride=rows), :].astype(BF16)
        edge[1, f] = plane[pl.ds(rows - 1, cols, stride=rows), :].astype(BF16)

    def act_frame(f, carry):
        taps = [clip[f + 2], clip[f + 1] * mask(f, 1), clip[f] * mask(f, 2)]
        taps = jnp.concatenate([tap.reshape(cols * rows, chans) for tap in taps], axis=1)
        value = jnp.dot(taps, t_fwd[...], preferred_element_type=F32).astype(BF16)
        act[f, 1 : cols + 1, :, chans : 2 * chans] = value.reshape(cols, rows, chans)
        edges_of(value, act_edge, f)
        return carry

    lax.fori_loop(0, frames, act_frame, 0)

    def halo_copies(edge, first, last, got_rows, got_cols, span, send, recv):
        parts = (
            (edge.at[0, span], got_rows.at[1, span]), (edge.at[1, span], got_rows.at[0, span]),
            (first, got_cols.at[1, 1, span]), (first, got_cols.at[1, 2, span]), (first, got_cols.at[1, 0, span]),
            (last, got_cols.at[0, 1, span]), (last, got_cols.at[0, 2, span]), (last, got_cols.at[0, 0, span]),
        )
        return [
            pltpu.make_async_remote_copy(
                src_ref=src, dst_ref=dst, send_sem=send.at[i], recv_sem=recv.at[i], device_id=around[i], device_id_type=MESH)
            for i, (src, dst) in enumerate(parts)
        ]

    mid = pl.ds(chans, chans)
    act_halo = halo_copies(
        act_edge, act.at[:, 1, :, mid], act.at[:, cols, :, mid], act_rows, act_cols, pl.ds(0, frames), a_send, a_recv)
    for copy in act_halo:
        copy.start()

    row = lax.broadcasted_iota(jnp.int32, (rows, chans), 0)
    is_first, is_last = row == 0, row == rows - 1
    has_up, has_down = h > 0, h < n_h - 1
    has_side = (block > 0, block < blocks - 1)

    def kept(flag, value):
        return jnp.where(flag, value, jnp.zeros_like(value))

    def shifted(middle, above, below):
        before = jnp.where(is_first, jnp.broadcast_to(above, middle.shape), pltpu.roll(middle, 1, 0))
        after = jnp.where(is_last, jnp.broadcast_to(below, middle.shape), pltpu.roll(middle, rows - 1, 0))
        return before.astype(BF16), after.astype(BF16)

    def with_halo(f, middle_of, got_rows, got_cols, put):
        above = kept(has_up, got_rows[0, f].astype(F32))
        below = kept(has_down, got_rows[1, f].astype(F32))
        for c in range(cols):
            middle = middle_of(c)
            before, after = shifted(middle.astype(F32), above[c : c + 1], below[c : c + 1])
            put(c + 1, before, middle, after)
        for side, c in ((0, 0), (1, cols + 1)):
            middle = kept(has_side[side], got_cols[side, 1, f].astype(F32))
            above_side = kept(has_side[side] & has_up, got_cols[side, 0, f].astype(F32))[rows - 1 : rows]
            below_side = kept(has_side[side] & has_down, got_cols[side, 2, f].astype(F32))[0:1]
            before, after = shifted(middle, above_side, below_side)
            put(c, before, middle.astype(BF16), after)

    for copy in act_halo:
        copy.wait()

    def slope_frame(f, carry):
        def put(c, before, middle, after):
            act[f, c, :, 0:chans] = before
            if c == 0 or c == cols + 1:
                act[f, c, :, chans : 2 * chans] = middle
            act[f, c, :, 2 * chans : 3 * chans] = after

        with_halo(f, lambda c: act[f, c + 1, :, chans : 2 * chans], act_rows, act_cols, put)
        wide_act = jnp.concatenate([act[f, b : b + cols].reshape(cols * rows, 3 * chans) for b in range(3)], axis=1)
        pre = jnp.dot(wide_act, s_fwd[...], preferred_element_type=F32)
        sig = jax.nn.sigmoid(pre)
        slope[f] = sig * (1.0 + pre * (1.0 - sig))
        return carry

    lax.fori_loop(0, frames, slope_frame, 0)

    def delta_halo(t):
        span = pl.ds(t * pair, pair)
        return halo_copies(
            delta_edge, delta.at[span, 0], delta.at[span, cols - 1], delta_rows, delta_cols, span, d_send.at[t], d_recv.at[t])

    own_grad.wait()

    def delta_pair(j, carry):
        d = step_of(j)
        t = (tm + n_tm - d) % n_tm

        @pl.when(j > 0)
        def _():
            vz_copy(d).wait()

        for i in range(pair):
            f = t * pair + i
            value = (grads[t, :, i].reshape(cols * rows, chans).astype(F32) * slope[f]).astype(BF16)
            delta[f] = value.reshape(cols, rows, chans)
            edges_of(value, delta_edge, f)
        for copy in delta_halo(t):
            copy.start()
        span = pl.ds(t * pair, pair)
        here = delta[span].reshape(pair * cols * rows, chans)
        for b in range(3):
            source = act[span, b : b + cols].reshape(pair * cols * rows, 3 * chans)
            s_total[:, b * 3 * chans : (b + 1) * 3 * chans] += lax.dot_general(
                here, source, (((0,), (0,)), ((), ())), preferred_element_type=F32)
        return carry

    lax.fori_loop(0, n_tm, delta_pair, 0)

    def back_pair(j, carry):
        t = (tm + n_tm - step_of(j)) % n_tm
        for copy in delta_halo(t):
            copy.wait()

        def back_frame(f, carry):
            def put(c, before, middle, after):
                wide[c, :, 0:chans] = after
                wide[c, :, chans : 2 * chans] = middle
                wide[c, :, 2 * chans : 3 * chans] = before

            with_halo(f, lambda c: delta[f, c], delta_rows, delta_cols, put)
            wide_delta = jnp.concatenate(
                [wide[2 - b : 2 - b + cols].reshape(cols * rows, 3 * chans) for b in range(3)], axis=1)
            act_grad[f] = jnp.dot(wide_delta, s_bwd[...], preferred_element_type=F32).astype(BF16)
            return carry

        return lax.fori_loop(t * pair, t * pair + pair, back_frame, carry)

    lax.fori_loop(0, n_tm, back_pair, 0)

    def time_frame(f, t_total):
        parts = [
            act_grad[f].reshape(cols, rows, chans),
            act_grad[f + 1].reshape(cols, rows, chans) * mask(f + 1, 1),
            act_grad[f + 2].reshape(cols, rows, chans) * mask(f + 2, 2),
        ]
        parts = jnp.concatenate([part.reshape(cols * rows, chans) for part in parts], axis=1)
        value = jnp.dot(parts, t_bwd[...], preferred_element_type=F32).astype(BF16)
        moved[f] = value.reshape(cols, rows, chans)
        here = clip[f + 2].reshape(cols * rows, chans)
        return t_total + lax.dot_general(here, parts, (((0,), (0,)), ((), ())), preferred_element_type=F32)

    t_total = lax.fori_loop(0, frames, time_frame, jnp.zeros((chans, 3 * chans), F32))

    def out_copy(d):
        to = (h + d) % n_h
        return pltpu.make_async_remote_copy(
            src_ref=moved.at[:, to], dst_ref=video_grad.at[0, 0, :, pl.ds(pl.multiple_of(h * rows, rows), rows)],
            send_sem=o_send.at[d], recv_sem=o_recv.at[d], device_id=(tm, to, w), device_id_type=MESH)

    lax.fori_loop(1, n_h, started(out_copy), 0)
    own_out = pltpu.make_async_copy(
        moved.at[:, h], video_grad.at[0, 0, :, pl.ds(pl.multiple_of(h * rows, rows), rows)], local_sem.at[2])
    own_out.start()

    for a in range(3):
        for b in range(3):
            terms[pl.ds((a * 3 + b) * chans, chans), :] = (
                s_total[:, (b * 3 + a) * chans : (b * 3 + a + 1) * chans].T * scale)
    for k in range(3):
        terms[pl.ds((9 + k) * chans, chans), :] = t_total[:, k * chans : (k + 1) * chans] * scale

    half_rows = half.shape[0]
    piece = half_rows // n_h
    mine = pl.multiple_of(w * half_rows, half_rows)
    swap = pltpu.make_async_remote_copy(
        src_ref=terms.at[pl.ds(pl.multiple_of((1 - w) * half_rows, half_rows), half_rows)], dst_ref=pair_buf,
        send_sem=pair_sem.at[0], recv_sem=pair_sem.at[1], device_id=(tm, h, 1 - w), device_id_type=MESH)
    swap.start()
    swap.wait()
    half[...] = terms[pl.ds(mine, half_rows), :] + pair_buf[...]

    def h_copy(d):
        to = (h + d) % n_h
        return pltpu.make_async_remote_copy(
            src_ref=half.at[pl.ds(pl.multiple_of(to * piece, 8), piece)], dst_ref=h_buf.at[d],
            send_sem=h_send.at[d], recv_sem=h_recv.at[d], device_id=(tm, to, w), device_id_type=MESH)

    lax.fori_loop(1, n_h, started(h_copy), 0)
    lax.fori_loop(1, n_h, waited(h_copy), 0)
    total = half[pl.ds(pl.multiple_of(h * piece, 8), piece), :]
    for d in range(1, n_h):
        total = total + h_buf[d]
    z_buf[tm] = total

    def z_copy(d):
        return pltpu.make_async_remote_copy(
            src_ref=z_buf.at[tm], dst_ref=z_buf.at[tm],
            send_sem=z_send.at[d], recv_sem=z_recv.at[d], device_id=((tm + d) % n_tm, h, w), device_id_type=MESH)

    lax.fori_loop(1, n_tm, started(z_copy), 0)
    lax.fori_loop(1, n_tm, waited(z_copy), 0)
    total = z_buf[0]
    for t in range(1, n_tm):
        total = total + z_buf[t]
    here = pl.ds(pl.multiple_of(mine + h * piece, 8), piece)
    sums[here, :] = total

    def g_copy(d):
        return pltpu.make_async_remote_copy(
            src_ref=sums.at[here], dst_ref=sums.at[here],
            send_sem=g_send.at[d], recv_sem=g_recv.at[d], device_id=(tm, (h + d) % n_h, w), device_id_type=MESH)

    def f_copy(d):
        there = pl.ds(pl.multiple_of(mine + ((h + n_h - d) % n_h) * piece, 8), piece)
        return pltpu.make_async_remote_copy(
            src_ref=sums.at[there], dst_ref=sums.at[there],
            send_sem=f_send.at[d], recv_sem=f_recv.at[d], device_id=(tm, h, 1 - w), device_id_type=MESH)

    lax.fori_loop(1, n_h, started(g_copy), 0)
    f_copy(0).start()

    def forward(d, carry):
        g_copy(d).wait()
        f_copy(d).start()
        return carry

    lax.fori_loop(1, n_h, forward, 0)
    lax.fori_loop(0, n_h, waited(f_copy), 0)
    own_out.wait()
    lax.fori_loop(1, n_h, waited(out_copy), 0)


def shards(n_tm, n_h, n_w, video, out_grad, lengths, temporal_weight, spatial_weight):
    frames, all_rows, chans = video.shape[2:]
    rows = all_rows // n_h
    cols = out_grad.shape[1] // n_tm
    pair = frames // n_tm
    lags = temporal_weight.shape[0]
    offs = spatial_weight.shape[0]
    n_terms = (lags + offs * offs) * chans
    piece = n_terms // n_w // n_h
    scale = float(frames * all_rows * cols * n_tm * n_w) ** (-0.5)
    dma = pltpu.SemaphoreType.DMA
    vmem = pltpu.VMEM
    video_grad, sums = pl.pallas_call(
        functools.partial(kernel, n_tm, n_h, n_w, scale),
        out_shape=(jax.ShapeDtypeStruct(video.shape, BF16), jax.ShapeDtypeStruct((n_terms, chans), F32)),
        in_specs=[
            pl.BlockSpec(memory_space=pl.ANY),
            pl.BlockSpec(memory_space=pl.ANY),
            pl.BlockSpec(memory_space=pltpu.SMEM),
            pl.BlockSpec(memory_space=pltpu.VMEM),
            pl.BlockSpec(memory_space=pltpu.VMEM),
        ],
        out_specs=(pl.BlockSpec(memory_space=pl.ANY), pl.BlockSpec(memory_space=pltpu.VMEM)),
        scratch_shapes=[
            vmem((frames + 2, cols, rows, chans), BF16),
            vmem((n_tm, cols, pair, rows, chans), BF16),
            vmem((frames, cols + 2, rows, 3 * chans), BF16),
            vmem((2, 3, frames, rows, chans), BF16),
            vmem((2, frames, cols, chans), BF16),
            vmem((2, frames, cols, chans), BF16),
            vmem((frames, cols, rows, chans), BF16),
            vmem((2, 3, frames, rows, chans), BF16),
            vmem((2, frames, cols, chans), BF16),
            vmem((2, frames, cols, chans), BF16),
            vmem((frames, cols * rows, chans), F32),
            vmem((frames + 2, cols * rows, chans), BF16),
            vmem((frames, cols, rows, chans), BF16),
            vmem((cols * rows, chans), F32),
            vmem((cols + 2, rows, 3 * chans), BF16),
            vmem((chans, offs * offs * chans), F32),
            vmem((n_terms, chans), F32),
            vmem((n_terms // 2, chans), F32),
            vmem((n_terms // 2, chans), F32),
            vmem((n_h, piece, chans), F32),
            vmem((n_tm, piece, chans), F32),
            vmem((lags * chans, chans), BF16),
            vmem((lags * chans, chans), BF16),
            vmem((offs * offs * chans, chans), BF16),
            vmem((offs * offs * chans, chans), BF16),
            dma((3,)), dma((n_tm,)), dma((n_tm,)), dma((n_h,)), dma((n_h,)), dma((8,)), dma((8,)), dma((n_tm, 8)), dma((n_tm, 8)),
            dma((n_h,)), dma((n_h,)),
            dma((2,)), dma((n_h,)), dma((n_h,)), dma((n_tm,)), dma((n_tm,)), dma((n_h,)), dma((n_h,)), dma((n_h,)), dma((n_h,)),
        ],
        compiler_params=pltpu.CompilerParams(collective_id=0, has_side_effects=True, vmem_limit_bytes=48 << 20),
    )(video, out_grad, lengths, temporal_weight, spatial_weight)
    split = offs * offs * chans
    return (
        video_grad,
        sums[split:].reshape(lags, chans, chans),
        sums[:split].reshape(offs, offs, chans, chans),
    )


def solution(mesh):
    placed = (
        P("width", ("tm", "height"), None, None, None),
        P("width", None, "tm", "height", None),
        P(),
        P(),
        P(),
    )
    return jax.shard_map(
        functools.partial(shards, mesh.shape["tm"], mesh.shape["height"], mesh.shape["width"]),
        mesh=mesh,
        in_specs=placed,
        out_specs=(P("width", ("tm", "height"), None, None, None), P(), P()),
        check_vma=False,
    )
```

```python
import functools

import jax
import jax.numpy as jnp
from jax import lax
from jax.experimental import pallas as pl
from jax.experimental.pallas import tpu as pltpu
from jax.sharding import PartitionSpec as P

MESH = pl.DeviceIdType.MESH
BF16 = jnp.bfloat16
F32 = jnp.float32


def started(copy):
    def body(d, carry):
        copy(d).start()
        return carry

    return body


def waited(copy):
    def body(d, carry):
        copy(d).wait()
        return carry

    return body


def kernel(
    n_tm, n_h, n_w, scale,
    video, out_grad, lengths_in, t_weight_in, s_weight_in,
    video_grad, t_out, s_out,
    clip, grads, act, act_got, act_sent, delta, delta_got, delta_sent,
    slope, act_grad, moved, plane, wide, s_total, t_total, s_bufs, t_bufs,
    t_fwd, t_bwd, s_fwd, s_bwd, lengths, t_weight, s_weight,
    local_sem, vz_send, vz_recv, vh_send, vh_recv, a_send, a_recv, d_send, d_recv, o_send, o_recv, s_sems, t_sems,
):
    tm = lax.axis_index("tm")
    h = lax.axis_index("height")
    w = lax.axis_index("width")
    frames, cols, rows, chans = delta.shape
    pair = frames // n_tm
    up, down = (h + n_h - 1) % n_h, (h + 1) % n_h
    block = w * n_tm + tm
    blocks = n_w * n_tm
    left, right = (block + blocks - 1) % blocks, (block + 1) % blocks
    left_tm, left_w = left % n_tm, left // n_tm
    right_tm, right_w = right % n_tm, right // n_tm
    around = (
        (tm, up, w), (tm, down, w), (left_tm, h, left_w), (right_tm, h, right_w),
        (left_tm, up, left_w), (left_tm, down, left_w), (right_tm, up, right_w), (right_tm, down, right_w),
    )

    loads = [
        pltpu.make_async_copy(src, dst, local_sem.at[i])
        for i, (src, dst) in enumerate(((t_weight_in, t_weight), (s_weight_in, s_weight), (lengths_in, lengths)))
    ]
    for load in loads:
        load.start()
    barrier = pltpu.get_barrier_semaphore()

    def greet_h(d, carry):
        pl.semaphore_signal(barrier, inc=1, device_id=(tm, (h + d) % n_h, w), device_id_type=MESH)
        return carry

    def greet_z(d, carry):
        pl.semaphore_signal(barrier, inc=1, device_id=((tm + d) % n_tm, h, w), device_id_type=MESH)
        return carry

    lax.fori_loop(1, n_tm, greet_z, 0)
    lax.fori_loop(1, n_h, greet_h, 0)
    pl.semaphore_signal(barrier, inc=1, device_id=(tm, h, 1 - w), device_id_type=MESH)
    for other in around[2:]:
        pl.semaphore_signal(barrier, inc=1, device_id=other, device_id_type=MESH)
    pl.semaphore_wait(barrier, n_tm - 1 + n_h - 1 + 1 + 6)

    def vz_copy(d):
        to = (tm + d) % n_tm
        return pltpu.make_async_remote_copy(
            src_ref=out_grad.at[0, pl.ds(to * cols, cols)], dst_ref=grads.at[tm],
            send_sem=vz_send.at[d], recv_sem=vz_recv.at[d], device_id=(to, h, w), device_id_type=MESH)

    def vh_copy(d):
        to = (h + d) % n_h
        return pltpu.make_async_remote_copy(
            src_ref=video.at[0, 0, :, pl.ds(pl.multiple_of(to * rows, rows), rows)], dst_ref=clip.at[h, pl.ds(2, frames)],
            send_sem=vh_send.at[d], recv_sem=vh_recv.at[d], device_id=(tm, to, w), device_id_type=MESH)

    def step_of(j):
        return (((j + 1) // 2) * (2 * (j % 2) - 1) + n_tm) % n_tm

    early = n_tm - 2
    lax.fori_loop(1, n_h, started(vh_copy), 0)
    lax.fori_loop(1, early, lambda j, carry: started(vz_copy)(step_of(j), carry), 0)
    own_grad = pltpu.make_async_copy(out_grad.at[0, pl.ds(tm * cols, cols)], grads.at[tm], local_sem.at[3])
    own_clip = pltpu.make_async_copy(
        video.at[0, 0, :, pl.ds(pl.multiple_of(h * rows, rows), rows)], clip.at[h, pl.ds(2, frames)], local_sem.at[4])
    own_grad.start()
    own_clip.start()

    for f in range(2):
        clip[:, f] = jnp.zeros((cols, rows, chans), BF16)
        act_grad[frames + f] = jnp.zeros((cols * rows, chans), BF16)
    for load in loads:
        load.wait()
    for k in range(3):
        t_fwd[k * chans : (k + 1) * chans, :] = t_weight[k]
        t_bwd[k * chans : (k + 1) * chans, :] = t_weight[k].T
    for b in range(3):
        for a in range(3):
            place = pl.ds((b * 3 + a) * chans, chans)
            s_fwd[place, :] = s_weight[a, b]
            s_bwd[place, :] = s_weight[a, b].T
    s_total[...] = jnp.zeros_like(s_total)
    t_total[...] = jnp.zeros_like(t_total)
    delta_sent[1][...] = jnp.zeros_like(delta_sent[1])
    starts = [lengths[0], lengths[0] + lengths[1], lengths[0] + lengths[1] + lengths[2]]

    def mask(f, lag):
        keep = jnp.where(f >= lag, 1, 0)
        for start in starts:
            keep = jnp.where((start > f - lag) & (start <= f), 0, keep)
        return jnp.broadcast_to(keep.astype(F32), (rows, chans)).astype(BF16)[None]

    own_clip.wait()
    lax.fori_loop(1, n_h, waited(vh_copy), 0)

    def edges_of(value, sent, corner_at, f, i):
        edge, corner = sent
        plane[i] = value.astype(F32)
        edge[0, f] = plane[i, pl.ds(0, cols, stride=rows), :].astype(BF16)
        edge[1, f] = plane[i, pl.ds(rows - 1, cols, stride=rows), :].astype(BF16)
        for k, place in enumerate((0, rows - 1, (cols - 1) * rows, cols * rows - 1)):
            corner[corner_at(k)] = plane[i, place : place + 1, :]

    def act_corner(f):
        return lambda k: (k, pl.ds(f, 1))

    def delta_corner(t, i):
        return lambda k: (k, t, pl.ds(i, 1))

    def flat(blocks):
        return [block.reshape(cols * rows, chans) for block in blocks]

    def act_pair(t, carry):
        lines = []
        for i in range(pair):
            f = t * pair + i
            lines.append(jnp.concatenate(flat([clip[:, f + 2], clip[:, f + 1] * mask(f, 1), clip[:, f] * mask(f, 2)]), axis=1))
        both = jnp.dot(jnp.concatenate(lines, axis=0), t_fwd[...], preferred_element_type=F32).astype(BF16)
        for i in range(pair):
            value = both[i * cols * rows : (i + 1) * cols * rows]
            act[t * pair + i, 1 : cols + 1, :, chans : 2 * chans] = value.reshape(cols, rows, chans)
            edges_of(value, act_sent, act_corner(t * pair + i), t * pair + i, i)
        return carry

    lax.fori_loop(0, n_tm, act_pair, 0)

    def halo_copies(sent, got, first, last, span, part, send, recv):
        (edge, corner), (got_rows, got_cols, got_corner) = sent, got
        parts = [
            (edge.at[0, span], got_rows.at[1, span]), (edge.at[1, span], got_rows.at[0, span]),
            (first, got_cols.at[1, span]), (last, got_cols.at[0, span]),
        ] + [(corner.at[(k, *part)], got_corner.at[(3 - k, *part)]) for k in range(4)]
        return [
            pltpu.make_async_remote_copy(
                src_ref=src, dst_ref=dst, send_sem=send.at[i], recv_sem=recv.at[i], device_id=around[i], device_id_type=MESH)
            for i, (src, dst) in enumerate(parts)
        ]

    mid = pl.ds(chans, chans)
    act_halo = halo_copies(
        act_sent, act_got, act.at[:, 1, :, mid], act.at[:, cols, :, mid], pl.ds(0, frames), (), a_send, a_recv)
    for copy in act_halo:
        copy.start()
    lax.fori_loop(early, n_tm, lambda j, carry: started(vz_copy)(step_of(j), carry), 0)

    row = lax.broadcasted_iota(jnp.int32, (rows, chans), 0)
    is_first, is_last = row == 0, row == rows - 1
    has_up, has_down = h > 0, h < n_h - 1
    has_side = (block > 0, block < blocks - 1)

    def kept(flag, value):
        return jnp.where(flag, value, jnp.zeros_like(value))

    def shifted(middle, above, below):
        before = jnp.where(is_first, jnp.broadcast_to(above, middle.shape), pltpu.roll(middle, 1, 0))
        after = jnp.where(is_last, jnp.broadcast_to(below, middle.shape), pltpu.roll(middle, rows - 1, 0))
        return before.astype(BF16), after.astype(BF16)

    def with_halo(f, middle_of, got, corner_at, put):
        got_rows, got_cols, got_corner = got
        above = kept(has_up, got_rows[0, f].astype(F32))
        below = kept(has_down, got_rows[1, f].astype(F32))
        for c in range(cols):
            middle = middle_of(c)
            before, after = shifted(middle.astype(F32), above[c : c + 1], below[c : c + 1])
            put(c + 1, before, middle, after)
        for side, c in ((0, 0), (1, cols + 1)):
            middle = kept(has_side[side], got_cols[side, f].astype(F32))
            above_side = kept(has_side[side] & has_up, got_corner[corner_at(2 * side)])
            below_side = kept(has_side[side] & has_down, got_corner[corner_at(2 * side + 1)])
            before, after = shifted(middle, above_side, below_side)
            put(c, before, middle.astype(BF16), after)

    for copy in act_halo:
        copy.wait()

    def slope_pair(t, carry):
        lines = []
        for i in range(pair):
            f = t * pair + i

            def put(c, before, middle, after):
                act[f, c, :, 0:chans] = before
                if c == 0 or c == cols + 1:
                    act[f, c, :, chans : 2 * chans] = middle
                act[f, c, :, 2 * chans : 3 * chans] = after

            with_halo(f, lambda c: act[f, c + 1, :, chans : 2 * chans], act_got, act_corner(f), put)
            lines.append(
                jnp.concatenate([act[f, b : b + cols].reshape(cols * rows, 3 * chans) for b in range(3)], axis=1))
        pre = jnp.dot(jnp.concatenate(lines, axis=0), s_fwd[...], preferred_element_type=F32)
        sig = jax.nn.sigmoid(pre)
        slope[pl.ds(t * pair, pair)] = (sig * (1.0 + pre * (1.0 - sig))).reshape(pair, cols * rows, chans)
        return carry

    lax.fori_loop(0, n_tm, slope_pair, 0)

    def delta_halo(t):
        span = pl.ds(t * pair, pair)
        return halo_copies(
            delta_sent, delta_got, delta.at[span, 0], delta.at[span, cols - 1], span, (t,), d_send.at[t], d_recv.at[t])

    own_grad.wait()

    def delta_pair(j):
        d = step_of(j)
        t = (tm + n_tm - d) % n_tm

        @pl.when(j > 0)
        def _():
            vz_copy(d).wait()

        for i in range(pair):
            f = t * pair + i
            value = (grads[t, :, i].reshape(cols * rows, chans).astype(F32) * slope[f]).astype(BF16)
            delta[f] = value.reshape(cols, rows, chans)
            edges_of(value, delta_sent, delta_corner(t, i), f, i)
        for copy in delta_halo(t):
            copy.start()
        span = pl.ds(t * pair, pair)
        here = delta[span].reshape(pair * cols * rows, chans)
        for b in range(3):
            source = act[span, b : b + cols].reshape(pair * cols * rows, 3 * chans)
            s_total[:, b * 3 * chans : (b + 1) * 3 * chans] += lax.dot_general(
                here, source, (((0,), (0,)), ((), ())), preferred_element_type=F32)

    def back_pair(j):
        t = (tm + n_tm - step_of(j)) % n_tm
        for copy in delta_halo(t):
            copy.wait()
        lines = []
        for i in range(pair):
            f = t * pair + i

            def put(c, before, middle, after):
                wide[i, c, :, 0:chans] = after
                wide[i, c, :, chans : 2 * chans] = middle
                wide[i, c, :, 2 * chans : 3 * chans] = before

            with_halo(f, lambda c: delta[f, c], delta_got, delta_corner(t, i), put)
            lines.append(jnp.concatenate(
                [wide[i, 2 - b : 2 - b + cols].reshape(cols * rows, 3 * chans) for b in range(3)], axis=1))
        value = jnp.dot(jnp.concatenate(lines, axis=0), s_bwd[...], preferred_element_type=F32).astype(BF16)
        act_grad[pl.ds(t * pair, pair)] = value.reshape(pair, cols * rows, chans)

    lag = 3

    def delta_back(j, carry):
        delta_pair(j)

        @pl.when(j >= lag)
        def _():
            back_pair(j - lag)

        return carry

    def back_only(j, carry):
        back_pair(j)
        return carry

    lax.fori_loop(0, n_tm, delta_back, 0)

    def device(t, row_band, core):
        return {"device_id": (t, row_band, core), "device_id_type": MESH}

    def summed_over_all(terms, out, bufs, sems):
        pair_buf, half, h_buf, z_buf = bufs
        swap_sem, h_send, h_recv, z_send, z_recv, g_send, g_recv, f_sem = sems
        taps = half.shape[0]
        piece = chans // n_h
        mine, theirs = pl.ds(w * taps, taps), pl.ds((1 - w) * taps, taps)

        def band(i):
            return pl.ds(pl.multiple_of(i * piece, piece), piece)

        swap = pltpu.make_async_remote_copy(
            src_ref=terms.at[theirs], dst_ref=pair_buf, send_sem=swap_sem.at[0], recv_sem=swap_sem.at[1],
            **device(tm, h, 1 - w))

        def h_copy(d):
            to = (h + d) % n_h
            return pltpu.make_async_remote_copy(
                src_ref=half.at[:, band(to)], dst_ref=h_buf.at[d], send_sem=h_send.at[d], recv_sem=h_recv.at[d],
                **device(tm, to, w))

        def z_copy(d):
            return pltpu.make_async_remote_copy(
                src_ref=z_buf.at[tm], dst_ref=z_buf.at[tm], send_sem=z_send.at[d], recv_sem=z_recv.at[d],
                **device((tm + d) % n_tm, h, w))

        def g_copy(d):
            return pltpu.make_async_remote_copy(
                src_ref=out.at[mine, band(h)], dst_ref=out.at[mine, band(h)], send_sem=g_send.at[d], recv_sem=g_recv.at[d],
                **device(tm, (h + d) % n_h, w))

        share = pltpu.make_async_remote_copy(
            src_ref=out.at[mine], dst_ref=out.at[mine], send_sem=f_sem.at[0], recv_sem=f_sem.at[1],
            **device(tm, h, 1 - w))

        def stage0():
            swap.start()

        def stage1():
            swap.wait()
            half[...] = terms[mine] + pair_buf[...]
            lax.fori_loop(1, n_h, started(h_copy), 0)

        def stage2():
            lax.fori_loop(1, n_h, waited(h_copy), 0)
            total = half[:, band(h), :]
            for d in range(1, n_h):
                total = total + h_buf[d]
            z_buf[tm] = total
            lax.fori_loop(1, n_tm, started(z_copy), 0)

        def stage3():
            lax.fori_loop(1, n_tm, waited(z_copy), 0)
            total = z_buf[0]
            for t in range(1, n_tm):
                total = total + z_buf[t]
            out[mine, band(h), :] = total
            lax.fori_loop(1, n_h, started(g_copy), 0)

        def stage4():
            lax.fori_loop(1, n_h, waited(g_copy), 0)
            share.start()

        def stage5():
            share.wait()

        return stage0, stage1, stage2, stage3, stage4, stage5

    s_terms, t_terms = s_bufs[0], t_bufs[0]
    s_stage = summed_over_all(s_terms, s_out, s_bufs[1:], s_sems)
    t_stage = summed_over_all(t_terms, t_out, t_bufs[1:], t_sems)
    for a in range(3):
        for b in range(3):
            s_terms[a * 3 + b] = s_total[:, (b * 3 + a) * chans : (b * 3 + a + 1) * chans].T * scale
    for k in range(9, s_terms.shape[0]):
        s_terms[k] = jnp.zeros((chans, chans), F32)
    s_stage[0]()

    lax.fori_loop(n_tm - lag, n_tm, back_only, 0)
    s_stage[1]()

    def parts_of(t):
        lines = []
        for i in range(pair):
            f = t * pair + i
            lines.append(jnp.concatenate([
                act_grad[f],
                (act_grad[f + 1].reshape(cols, rows, chans) * mask(f + 1, 1)).reshape(cols * rows, chans),
                (act_grad[f + 2].reshape(cols, rows, chans) * mask(f + 2, 2)).reshape(cols * rows, chans),
            ], axis=1))
        return lines

    def weight_pair(t, carry):
        here = jnp.concatenate(flat([clip[:, t * pair + 2 + i] for i in range(pair)]), axis=0)
        t_total[...] += lax.dot_general(
            here, jnp.concatenate(parts_of(t), axis=0), (((0,), (0,)), ((), ())), preferred_element_type=F32)
        return carry

    def video_pair(t, carry):
        value = jnp.dot(jnp.concatenate(parts_of(t), axis=0), t_bwd[...], preferred_element_type=F32).astype(BF16)
        for i in range(pair):
            moved[:, t * pair + i] = value[i * cols * rows : (i + 1) * cols * rows].reshape(cols, rows, chans)
        return carry

    chunks = o_send.shape[0]
    length = frames // chunks

    def out_place(i):
        return video_grad.at[0, 0, pl.ds(i * length, length), pl.ds(pl.multiple_of(h * rows, rows), rows)]

    def out_copy(i):
        def copy(d):
            to = (h + d) % n_h
            return pltpu.make_async_remote_copy(
                src_ref=moved.at[to, pl.ds(i * length, length)], dst_ref=out_place(i),
                send_sem=o_send.at[i, d], recv_sem=o_recv.at[i, d], **device(tm, to, w))

        return copy

    def own_out(i):
        return pltpu.make_async_copy(moved.at[h, pl.ds(i * length, length)], out_place(i), local_sem.at[5 + i])

    lax.fori_loop(0, n_tm, weight_pair, 0)
    for k in range(3):
        t_terms[k] = t_total[:, k * chans : (k + 1) * chans] * scale
    for k in range(3, t_terms.shape[0]):
        t_terms[k] = jnp.zeros((chans, chans), F32)
    t_stage[0]()
    s_stage[2]()
    between = {0: t_stage[1], 1: s_stage[3], 2: t_stage[2]}
    for i in range(chunks):
        lax.fori_loop(i * n_tm // chunks, (i + 1) * n_tm // chunks, video_pair, 0)
        if i in between:
            between[i]()
        lax.fori_loop(1, n_h, started(out_copy(i)), 0)
        own_out(i).start()
    t_stage[3]()
    s_stage[4]()
    t_stage[4]()
    s_stage[5]()
    for i in range(chunks):
        own_out(i).wait()
        lax.fori_loop(1, n_h, waited(out_copy(i)), 0)
    t_stage[5]()


def shards(n_tm, n_h, n_w, video, out_grad, lengths, temporal_weight, spatial_weight):
    frames, all_rows, chans = video.shape[2:]
    rows = all_rows // n_h
    cols = out_grad.shape[1] // n_tm
    pair = frames // n_tm
    lags = temporal_weight.shape[0]
    offs = spatial_weight.shape[0]
    s_taps = -(-offs * offs // n_w)
    t_taps = -(-lags // n_w)
    chunks = 4
    scale = float(frames * all_rows * cols * n_tm * n_w) ** (-0.5)
    dma = pltpu.SemaphoreType.DMA
    vmem = pltpu.VMEM

    def sum_bufs(taps):
        return [
            vmem((n_w * taps, chans, chans), F32),
            vmem((taps, chans, chans), F32),
            vmem((taps, chans, chans), F32),
            vmem((n_h, taps, chans // n_h, chans), F32),
            vmem((n_tm, taps, chans // n_h, chans), F32),
        ]

    def sum_sems():
        return [dma((2,)), dma((n_h,)), dma((n_h,)), dma((n_tm,)), dma((n_tm,)), dma((n_h,)), dma((n_h,)), dma((2,))]

    hbm = pl.BlockSpec(memory_space=pltpu.HBM)
    video_grad, t_sum, s_sum = pl.pallas_call(
        functools.partial(kernel, n_tm, n_h, n_w, scale),
        out_shape=(
            jax.ShapeDtypeStruct(video.shape, BF16),
            jax.ShapeDtypeStruct((n_w * t_taps, chans, chans), F32),
            jax.ShapeDtypeStruct((n_w * s_taps, chans, chans), F32),
        ),
        in_specs=[hbm] * 5,
        out_specs=(
            pl.BlockSpec(memory_space=pl.ANY), pl.BlockSpec(memory_space=pltpu.VMEM), pl.BlockSpec(memory_space=pltpu.VMEM)),
        scratch_shapes=[
            vmem((cols, frames + 2, rows, chans), BF16),
            vmem((n_tm, cols, pair, rows, chans), BF16),
            vmem((frames, cols + 2, rows, 3 * chans), BF16),
            [vmem((2, frames, cols, chans), BF16), vmem((2, frames, rows, chans), BF16), vmem((4, frames, chans), F32)],
            [vmem((2, frames, cols, chans), BF16), vmem((4, frames, chans), F32)],
            vmem((frames, cols, rows, chans), BF16),
            [vmem((2, frames, cols, chans), BF16), vmem((2, frames, rows, chans), BF16), vmem((4, n_tm, 8, chans), F32)],
            [vmem((2, frames, cols, chans), BF16), vmem((4, n_tm, 8, chans), F32)],
            vmem((frames, cols * rows, chans), F32),
            vmem((frames + 2, cols * rows, chans), BF16),
            vmem((cols, frames, rows, chans), BF16),
            vmem((pair, cols * rows, chans), F32),
            vmem((pair, cols + 2, rows, 3 * chans), BF16),
            vmem((chans, offs * offs * chans), F32),
            vmem((chans, lags * chans), F32),
            sum_bufs(s_taps),
            sum_bufs(t_taps),
            vmem((lags * chans, chans), BF16),
            vmem((lags * chans, chans), BF16),
            vmem((offs * offs * chans, chans), BF16),
            vmem((offs * offs * chans, chans), BF16),
            pltpu.SMEM(lengths.shape, jnp.int32),
            vmem(temporal_weight.shape, BF16),
            vmem(spatial_weight.shape, BF16),
            dma((5 + chunks,)), dma((n_tm,)), dma((n_tm,)), dma((n_h,)), dma((n_h,)), dma((8,)), dma((8,)),
            dma((n_tm, 8)), dma((n_tm, 8)), dma((chunks, n_h)), dma((chunks, n_h)),
            sum_sems(),
            sum_sems(),
        ],
        compiler_params=pltpu.CompilerParams(collective_id=0, has_side_effects=True, vmem_limit_bytes=48 << 20),
    )(video, out_grad, lengths, temporal_weight, spatial_weight)
    return (
        video_grad,
        t_sum[:lags],
        s_sum[: offs * offs].reshape(offs, offs, chans, chans),
    )


def solution(mesh):
    placed = (
        P("width", ("tm", "height"), None, None, None),
        P("width", None, "tm", "height", None),
        P(),
        P(),
        P(),
    )
    return jax.shard_map(
        functools.partial(shards, mesh.shape["tm"], mesh.shape["height"], mesh.shape["width"]),
        mesh=mesh,
        in_specs=placed,
        out_specs=(P("width", ("tm", "height"), None, None, None), P(), P()),
        check_vma=False,
    )
```

```python
import functools

import jax
import jax.numpy as jnp
from jax import lax
from jax.experimental import pallas as pl
from jax.experimental.pallas import tpu as pltpu
from jax.sharding import PartitionSpec as P

MESH = pl.DeviceIdType.MESH
BF16 = jnp.bfloat16
F32 = jnp.float32


def started(copy):
    def body(d, carry):
        copy(d).start()
        return carry

    return body


def waited(copy):
    def body(d, carry):
        copy(d).wait()
        return carry

    return body


def kernel(
    n_tm, n_h, n_w, scale,
    video, out_grad, lengths_in, t_weight_in, s_weight_in,
    video_grad, t_out, s_out,
    clip, grads, act, act_got, act_sent, delta, delta_got, delta_sent,
    slope, act_grad, moved, plane, wide, s_total, t_total, s_bufs, t_bufs,
    t_fwd, t_bwd, s_fwd, s_bwd, lengths, t_weight, s_weight,
    local_sem, vz_send, vz_recv, vh_send, vh_recv, a_send, a_recv, d_send, d_recv, o_send, o_recv, s_sems, t_sems,
):
    tm = lax.axis_index("tm")
    h = lax.axis_index("height")
    w = lax.axis_index("width")
    frames, cols, rows, chans = delta.shape
    pair = frames // n_tm
    up, down = (h + n_h - 1) % n_h, (h + 1) % n_h
    block = w * n_tm + tm
    blocks = n_w * n_tm
    left, right = (block + blocks - 1) % blocks, (block + 1) % blocks
    left_tm, left_w = left % n_tm, left // n_tm
    right_tm, right_w = right % n_tm, right // n_tm
    around = (
        (tm, up, w), (tm, down, w), (left_tm, h, left_w), (right_tm, h, right_w),
        (left_tm, up, left_w), (left_tm, down, left_w), (right_tm, up, right_w), (right_tm, down, right_w),
    )

    loads = [
        pltpu.make_async_copy(src, dst, local_sem.at[i])
        for i, (src, dst) in enumerate(((t_weight_in, t_weight), (s_weight_in, s_weight), (lengths_in, lengths)))
    ]
    for load in loads:
        load.start()
    barrier = pltpu.get_barrier_semaphore()

    def greet_h(d, carry):
        pl.semaphore_signal(barrier, inc=1, device_id=(tm, (h + d) % n_h, w), device_id_type=MESH)
        return carry

    def greet_z(d, carry):
        pl.semaphore_signal(barrier, inc=1, device_id=((tm + d) % n_tm, h, w), device_id_type=MESH)
        return carry

    lax.fori_loop(1, n_tm, greet_z, 0)
    lax.fori_loop(1, n_h, greet_h, 0)
    pl.semaphore_signal(barrier, inc=1, device_id=(tm, h, 1 - w), device_id_type=MESH)
    for other in around[2:]:
        pl.semaphore_signal(barrier, inc=1, device_id=other, device_id_type=MESH)
    pl.semaphore_wait(barrier, n_tm - 1 + n_h - 1 + 1 + 6)

    def vz_copy(d):
        to = (tm + d) % n_tm
        return pltpu.make_async_remote_copy(
            src_ref=out_grad.at[0, pl.ds(to * cols, cols)], dst_ref=grads.at[tm],
            send_sem=vz_send.at[d], recv_sem=vz_recv.at[d], device_id=(to, h, w), device_id_type=MESH)

    def vh_copy(d):
        to = (h + d) % n_h
        return pltpu.make_async_remote_copy(
            src_ref=video.at[0, 0, :, pl.ds(pl.multiple_of(to * rows, rows), rows)], dst_ref=clip.at[h, pl.ds(2, frames)],
            send_sem=vh_send.at[d], recv_sem=vh_recv.at[d], device_id=(tm, to, w), device_id_type=MESH)

    def step_of(j):
        return (((j + 1) // 2) * (2 * (j % 2) - 1) + n_tm) % n_tm

    lax.fori_loop(1, n_h, started(vh_copy), 0)
    lax.fori_loop(1, n_tm, lambda j, carry: started(vz_copy)(step_of(j), carry), 0)
    own_grad = pltpu.make_async_copy(out_grad.at[0, pl.ds(tm * cols, cols)], grads.at[tm], local_sem.at[3])
    own_clip = pltpu.make_async_copy(
        video.at[0, 0, :, pl.ds(pl.multiple_of(h * rows, rows), rows)], clip.at[h, pl.ds(2, frames)], local_sem.at[4])
    own_grad.start()
    own_clip.start()

    for f in range(2):
        clip[:, f] = jnp.zeros((cols, rows, chans), BF16)
        act_grad[frames + f] = jnp.zeros((cols * rows, chans), BF16)
    for load in loads:
        load.wait()
    for k in range(3):
        t_fwd[k * chans : (k + 1) * chans, :] = t_weight[k]
        t_bwd[k * chans : (k + 1) * chans, :] = t_weight[k].T
    for b in range(3):
        for a in range(3):
            place = pl.ds((b * 3 + a) * chans, chans)
            s_fwd[place, :] = s_weight[a, b]
            s_bwd[place, :] = s_weight[a, b].T
    s_total[...] = jnp.zeros_like(s_total)
    t_total[...] = jnp.zeros_like(t_total)
    delta_sent[1][...] = jnp.zeros_like(delta_sent[1])
    starts = [lengths[0], lengths[0] + lengths[1], lengths[0] + lengths[1] + lengths[2]]

    def mask(f, lag):
        keep = jnp.where(f >= lag, 1, 0)
        for start in starts:
            keep = jnp.where((start > f - lag) & (start <= f), 0, keep)
        return jnp.broadcast_to(keep.astype(F32), (rows, chans)).astype(BF16)[None]

    own_clip.wait()
    lax.fori_loop(1, n_h, waited(vh_copy), 0)

    def edges_of(value, sent, corner_at, f, i):
        edge, corner = sent
        plane[i] = value.astype(F32)
        edge[0, f] = plane[i, pl.ds(0, cols, stride=rows), :].astype(BF16)
        edge[1, f] = plane[i, pl.ds(rows - 1, cols, stride=rows), :].astype(BF16)
        for k, place in enumerate((0, rows - 1, (cols - 1) * rows, cols * rows - 1)):
            corner[corner_at(k)] = plane[i, place : place + 1, :]

    def act_corner(f):
        return lambda k: (k, pl.ds(f, 1))

    def delta_corner(t, i):
        return lambda k: (k, t, pl.ds(i, 1))

    def flat(blocks):
        return [block.reshape(cols * rows, chans) for block in blocks]

    def act_pair(t, carry):
        lines = []
        for i in range(pair):
            f = t * pair + i
            lines.append(jnp.concatenate(flat([clip[:, f + 2], clip[:, f + 1] * mask(f, 1), clip[:, f] * mask(f, 2)]), axis=1))
        both = jnp.dot(jnp.concatenate(lines, axis=0), t_fwd[...], preferred_element_type=F32).astype(BF16)
        for i in range(pair):
            value = both[i * cols * rows : (i + 1) * cols * rows]
            act[t * pair + i, 1 : cols + 1, :, chans : 2 * chans] = value.reshape(cols, rows, chans)
            edges_of(value, act_sent, act_corner(t * pair + i), t * pair + i, i)
        return carry

    lax.fori_loop(0, n_tm, act_pair, 0)

    def halo_copies(sent, got, first, last, span, part, send, recv):
        (edge, corner), (got_rows, got_cols, got_corner) = sent, got
        parts = [
            (edge.at[0, span], got_rows.at[1, span]), (edge.at[1, span], got_rows.at[0, span]),
            (first, got_cols.at[1, span]), (last, got_cols.at[0, span]),
        ] + [(corner.at[(k, *part)], got_corner.at[(3 - k, *part)]) for k in range(4)]
        return [
            pltpu.make_async_remote_copy(
                src_ref=src, dst_ref=dst, send_sem=send.at[i], recv_sem=recv.at[i], device_id=around[i], device_id_type=MESH)
            for i, (src, dst) in enumerate(parts)
        ]

    mid = pl.ds(chans, chans)
    act_halo = halo_copies(
        act_sent, act_got, act.at[:, 1, :, mid], act.at[:, cols, :, mid], pl.ds(0, frames), (), a_send, a_recv)
    for copy in act_halo:
        copy.start()

    row = lax.broadcasted_iota(jnp.int32, (rows, chans), 0)
    is_first, is_last = row == 0, row == rows - 1
    has_up, has_down = h > 0, h < n_h - 1
    has_side = (block > 0, block < blocks - 1)

    def kept(flag, value):
        return jnp.where(flag, value, jnp.zeros_like(value))

    def shifted(middle, above, below):
        before = jnp.where(is_first, jnp.broadcast_to(above, middle.shape), pltpu.roll(middle, 1, 0))
        after = jnp.where(is_last, jnp.broadcast_to(below, middle.shape), pltpu.roll(middle, rows - 1, 0))
        return before.astype(BF16), after.astype(BF16)

    def with_halo(f, middle_of, got, corner_at, put):
        got_rows, got_cols, got_corner = got
        above = kept(has_up, got_rows[0, f].astype(F32))
        below = kept(has_down, got_rows[1, f].astype(F32))
        for c in range(cols):
            middle = middle_of(c)
            before, after = shifted(middle.astype(F32), above[c : c + 1], below[c : c + 1])
            put(c + 1, before, middle, after)
        for side, c in ((0, 0), (1, cols + 1)):
            middle = kept(has_side[side], got_cols[side, f].astype(F32))
            above_side = kept(has_side[side] & has_up, got_corner[corner_at(2 * side)])
            below_side = kept(has_side[side] & has_down, got_corner[corner_at(2 * side + 1)])
            before, after = shifted(middle, above_side, below_side)
            put(c, before, middle.astype(BF16), after)

    for copy in act_halo:
        copy.wait()

    def slope_pair(t, carry):
        lines = []
        for i in range(pair):
            f = t * pair + i

            def put(c, before, middle, after):
                act[f, c, :, 0:chans] = before
                if c == 0 or c == cols + 1:
                    act[f, c, :, chans : 2 * chans] = middle
                act[f, c, :, 2 * chans : 3 * chans] = after

            with_halo(f, lambda c: act[f, c + 1, :, chans : 2 * chans], act_got, act_corner(f), put)
            lines.append(
                jnp.concatenate([act[f, b : b + cols].reshape(cols * rows, 3 * chans) for b in range(3)], axis=1))
        pre = jnp.dot(jnp.concatenate(lines, axis=0), s_fwd[...], preferred_element_type=F32)
        sig = jax.nn.sigmoid(pre)
        slope[pl.ds(t * pair, pair)] = (sig * (1.0 + pre * (1.0 - sig))).reshape(pair, cols * rows, chans)
        return carry

    lax.fori_loop(0, n_tm, slope_pair, 0)

    def delta_halo(t):
        span = pl.ds(t * pair, pair)
        return halo_copies(
            delta_sent, delta_got, delta.at[span, 0], delta.at[span, cols - 1], span, (t,), d_send.at[t], d_recv.at[t])

    own_grad.wait()

    def delta_pair(j, carry):
        d = step_of(j)
        t = (tm + n_tm - d) % n_tm

        @pl.when(j > 0)
        def _():
            vz_copy(d).wait()

        for i in range(pair):
            f = t * pair + i
            value = (grads[t, :, i].reshape(cols * rows, chans).astype(F32) * slope[f]).astype(BF16)
            delta[f] = value.reshape(cols, rows, chans)
            edges_of(value, delta_sent, delta_corner(t, i), f, i)
        for copy in delta_halo(t):
            copy.start()
        return carry

    def spatial_pair(t, carry):
        span = pl.ds(t * pair, pair)
        here = delta[span].reshape(pair * cols * rows, chans)
        for b in range(3):
            source = act[span, b : b + cols].reshape(pair * cols * rows, 3 * chans)
            s_total[:, b * 3 * chans : (b + 1) * 3 * chans] += lax.dot_general(
                here, source, (((0,), (0,)), ((), ())), preferred_element_type=F32)
        return carry

    def back_pair(j, carry):
        t = (tm + n_tm - step_of(j)) % n_tm
        for copy in delta_halo(t):
            copy.wait()
        lines = []
        for i in range(pair):
            f = t * pair + i

            def put(c, before, middle, after):
                wide[i, c, :, 0:chans] = after
                wide[i, c, :, chans : 2 * chans] = middle
                wide[i, c, :, 2 * chans : 3 * chans] = before

            with_halo(f, lambda c: delta[f, c], delta_got, delta_corner(t, i), put)
            lines.append(jnp.concatenate(
                [wide[i, 2 - b : 2 - b + cols].reshape(cols * rows, 3 * chans) for b in range(3)], axis=1))
        value = jnp.dot(jnp.concatenate(lines, axis=0), s_bwd[...], preferred_element_type=F32).astype(BF16)
        act_grad[pl.ds(t * pair, pair)] = value.reshape(pair, cols * rows, chans)
        return carry

    lax.fori_loop(0, n_tm, delta_pair, 0)
    lax.fori_loop(0, n_tm, spatial_pair, 0)

    def device(t, row_band, core):
        return {"device_id": (t, row_band, core), "device_id_type": MESH}

    def summed_over_all(terms, out, bufs, sems):
        pair_buf, half, h_buf, z_buf, got_mine, got_theirs = bufs
        swap_sem, h_send, h_recv, z_send, z_recv, g_send, g_recv, f_sem = sems
        taps = half.shape[0]
        piece = chans // n_h
        mine, theirs = pl.ds(w * taps, taps), pl.ds((1 - w) * taps, taps)

        def band(i):
            return pl.ds(pl.multiple_of(i * piece, piece), piece)

        swap = pltpu.make_async_remote_copy(
            src_ref=terms.at[theirs], dst_ref=pair_buf, send_sem=swap_sem.at[0], recv_sem=swap_sem.at[1],
            **device(tm, h, 1 - w))

        def h_copy(d):
            to = (h + d) % n_h
            return pltpu.make_async_remote_copy(
                src_ref=half.at[:, band(to)], dst_ref=h_buf.at[d], send_sem=h_send.at[d], recv_sem=h_recv.at[d],
                **device(tm, to, w))

        def z_copy(d):
            return pltpu.make_async_remote_copy(
                src_ref=z_buf.at[tm], dst_ref=z_buf.at[tm], send_sem=z_send.at[d], recv_sem=z_recv.at[d],
                **device((tm + d) % n_tm, h, w))

        def g_copy(d):
            return pltpu.make_async_remote_copy(
                src_ref=got_mine.at[h], dst_ref=got_mine.at[h], send_sem=g_send.at[d], recv_sem=g_recv.at[d],
                **device(tm, (h + d) % n_h, w))

        share = pltpu.make_async_remote_copy(
            src_ref=got_mine, dst_ref=got_theirs, send_sem=f_sem.at[0], recv_sem=f_sem.at[1],
            **device(tm, h, 1 - w))

        def stage0():
            swap.start()

        def stage1():
            swap.wait()
            half[...] = terms[mine] + pair_buf[...]
            lax.fori_loop(1, n_h, started(h_copy), 0)

        def stage2():
            lax.fori_loop(1, n_h, waited(h_copy), 0)
            total = half[:, band(h), :]
            for d in range(1, n_h):
                total = total + h_buf[d]
            z_buf[tm] = total
            lax.fori_loop(1, n_tm, started(z_copy), 0)

        def stage3():
            lax.fori_loop(1, n_tm, waited(z_copy), 0)
            total = z_buf[0]
            for t in range(1, n_tm):
                total = total + z_buf[t]
            got_mine[h] = total.astype(BF16)
            lax.fori_loop(1, n_h, started(g_copy), 0)

        def stage4():
            lax.fori_loop(1, n_h, waited(g_copy), 0)
            share.start()
            for i in range(n_h):
                out[mine, i * piece : (i + 1) * piece, :] = got_mine[i].astype(F32)

        def stage5():
            share.wait()
            for i in range(n_h):
                out[theirs, i * piece : (i + 1) * piece, :] = got_theirs[i].astype(F32)

        return stage0, stage1, stage2, stage3, stage4, stage5

    s_terms, t_terms = s_bufs[0], t_bufs[0]
    s_stage = summed_over_all(s_terms, s_out, s_bufs[1:], s_sems)
    t_stage = summed_over_all(t_terms, t_out, t_bufs[1:], t_sems)
    for a in range(3):
        for b in range(3):
            s_terms[a * 3 + b] = s_total[:, (b * 3 + a) * chans : (b * 3 + a + 1) * chans].T * scale
    for k in range(9, s_terms.shape[0]):
        s_terms[k] = jnp.zeros((chans, chans), F32)
    s_stage[0]()

    lax.fori_loop(0, n_tm // 2, back_pair, 0)
    s_stage[1]()
    lax.fori_loop(n_tm // 2, n_tm, back_pair, 0)

    def parts_of(t):
        lines = []
        for i in range(pair):
            f = t * pair + i
            lines.append(jnp.concatenate([
                act_grad[f],
                (act_grad[f + 1].reshape(cols, rows, chans) * mask(f + 1, 1)).reshape(cols * rows, chans),
                (act_grad[f + 2].reshape(cols, rows, chans) * mask(f + 2, 2)).reshape(cols * rows, chans),
            ], axis=1))
        return lines

    def weight_pair(t, carry):
        here = jnp.concatenate(flat([clip[:, t * pair + 2 + i] for i in range(pair)]), axis=0)
        t_total[...] += lax.dot_general(
            here, jnp.concatenate(parts_of(t), axis=0), (((0,), (0,)), ((), ())), preferred_element_type=F32)
        return carry

    def video_pair(t, carry):
        value = jnp.dot(jnp.concatenate(parts_of(t), axis=0), t_bwd[...], preferred_element_type=F32).astype(BF16)
        for i in range(pair):
            moved[:, t * pair + i] = value[i * cols * rows : (i + 1) * cols * rows].reshape(cols, rows, chans)
        return carry

    chunks = o_send.shape[0]
    length = frames // chunks

    def out_place(i):
        return video_grad.at[0, 0, pl.ds(i * length, length), pl.ds(pl.multiple_of(h * rows, rows), rows)]

    def out_copy(i):
        def copy(d):
            to = (h + d) % n_h
            return pltpu.make_async_remote_copy(
                src_ref=moved.at[to, pl.ds(i * length, length)], dst_ref=out_place(i),
                send_sem=o_send.at[i, d], recv_sem=o_recv.at[i, d], **device(tm, to, w))

        return copy

    def own_out(i):
        return pltpu.make_async_copy(moved.at[h, pl.ds(i * length, length)], out_place(i), local_sem.at[5 + i])

    lax.fori_loop(0, n_tm // 2, weight_pair, 0)
    s_stage[2]()
    lax.fori_loop(n_tm // 2, n_tm, weight_pair, 0)
    for k in range(3):
        t_terms[k] = t_total[:, k * chans : (k + 1) * chans] * scale
    for k in range(3, t_terms.shape[0]):
        t_terms[k] = jnp.zeros((chans, chans), F32)
    t_stage[0]()
    between = {0: s_stage[3], 1: t_stage[1], 3: t_stage[2]}
    for i in range(chunks):
        lax.fori_loop(i * n_tm // chunks, (i + 1) * n_tm // chunks, video_pair, 0)
        if i in between:
            between[i]()
        lax.fori_loop(1, n_h, started(out_copy(i)), 0)
        own_out(i).start()
    s_stage[4]()
    t_stage[3]()
    s_stage[5]()
    t_stage[4]()
    for i in range(chunks):
        own_out(i).wait()
        lax.fori_loop(1, n_h, waited(out_copy(i)), 0)
    t_stage[5]()


def shards(n_tm, n_h, n_w, video, out_grad, lengths, temporal_weight, spatial_weight):
    frames, all_rows, chans = video.shape[2:]
    rows = all_rows // n_h
    cols = out_grad.shape[1] // n_tm
    pair = frames // n_tm
    lags = temporal_weight.shape[0]
    offs = spatial_weight.shape[0]
    s_taps = -(-offs * offs // n_w)
    t_taps = -(-lags // n_w)
    chunks = 4
    scale = float(frames * all_rows * cols * n_tm * n_w) ** (-0.5)
    dma = pltpu.SemaphoreType.DMA
    vmem = pltpu.VMEM

    def sum_bufs(taps):
        return [
            vmem((n_w * taps, chans, chans), F32),
            vmem((taps, chans, chans), F32),
            vmem((taps, chans, chans), F32),
            vmem((n_h, taps, chans // n_h, chans), F32),
            vmem((n_tm, taps, chans // n_h, chans), F32),
            vmem((n_h, taps, chans // n_h, chans), BF16),
            vmem((n_h, taps, chans // n_h, chans), BF16),
        ]

    def sum_sems():
        return [dma((2,)), dma((n_h,)), dma((n_h,)), dma((n_tm,)), dma((n_tm,)), dma((n_h,)), dma((n_h,)), dma((2,))]

    hbm = pl.BlockSpec(memory_space=pltpu.HBM)
    video_grad, t_sum, s_sum = pl.pallas_call(
        functools.partial(kernel, n_tm, n_h, n_w, scale),
        out_shape=(
            jax.ShapeDtypeStruct(video.shape, BF16),
            jax.ShapeDtypeStruct((n_w * t_taps, chans, chans), F32),
            jax.ShapeDtypeStruct((n_w * s_taps, chans, chans), F32),
        ),
        in_specs=[hbm] * 5,
        out_specs=(
            pl.BlockSpec(memory_space=pl.ANY), pl.BlockSpec(memory_space=pltpu.VMEM), pl.BlockSpec(memory_space=pltpu.VMEM)),
        scratch_shapes=[
            vmem((cols, frames + 2, rows, chans), BF16),
            vmem((n_tm, cols, pair, rows, chans), BF16),
            vmem((frames, cols + 2, rows, 3 * chans), BF16),
            [vmem((2, frames, cols, chans), BF16), vmem((2, frames, rows, chans), BF16), vmem((4, frames, chans), F32)],
            [vmem((2, frames, cols, chans), BF16), vmem((4, frames, chans), F32)],
            vmem((frames, cols, rows, chans), BF16),
            [vmem((2, frames, cols, chans), BF16), vmem((2, frames, rows, chans), BF16), vmem((4, n_tm, 8, chans), F32)],
            [vmem((2, frames, cols, chans), BF16), vmem((4, n_tm, 8, chans), F32)],
            vmem((frames, cols * rows, chans), F32),
            vmem((frames + 2, cols * rows, chans), BF16),
            vmem((cols, frames, rows, chans), BF16),
            vmem((pair, cols * rows, chans), F32),
            vmem((pair, cols + 2, rows, 3 * chans), BF16),
            vmem((chans, offs * offs * chans), F32),
            vmem((chans, lags * chans), F32),
            sum_bufs(s_taps),
            sum_bufs(t_taps),
            vmem((lags * chans, chans), BF16),
            vmem((lags * chans, chans), BF16),
            vmem((offs * offs * chans, chans), BF16),
            vmem((offs * offs * chans, chans), BF16),
            pltpu.SMEM(lengths.shape, jnp.int32),
            vmem(temporal_weight.shape, BF16),
            vmem(spatial_weight.shape, BF16),
            dma((5 + chunks,)), dma((n_tm,)), dma((n_tm,)), dma((n_h,)), dma((n_h,)), dma((8,)), dma((8,)),
            dma((n_tm, 8)), dma((n_tm, 8)), dma((chunks, n_h)), dma((chunks, n_h)),
            sum_sems(),
            sum_sems(),
        ],
        compiler_params=pltpu.CompilerParams(collective_id=0, has_side_effects=True, vmem_limit_bytes=54 << 20),
    )(video, out_grad, lengths, temporal_weight, spatial_weight)
    return (
        video_grad,
        t_sum[:lags],
        s_sum[: offs * offs].reshape(offs, offs, chans, chans),
    )


def solution(mesh):
    placed = (
        P("width", ("tm", "height"), None, None, None),
        P("width", None, "tm", "height", None),
        P(),
        P(),
        P(),
    )
    return jax.shard_map(
        functools.partial(shards, mesh.shape["tm"], mesh.shape["height"], mesh.shape["width"]),
        mesh=mesh,
        in_specs=placed,
        out_specs=(P("width", ("tm", "height"), None, None, None), P(), P()),
        check_vma=False,
    )
```

```python
import functools

import jax
import jax.numpy as jnp
from jax import lax
from jax.experimental import pallas as pl
from jax.experimental.pallas import tpu as pltpu
from jax.sharding import PartitionSpec as P

MESH = pl.DeviceIdType.MESH
BF16 = jnp.bfloat16
F32 = jnp.float32


def started(copy):
    def body(d, carry):
        copy(d).start()
        return carry

    return body


def waited(copy):
    def body(d, carry):
        copy(d).wait()
        return carry

    return body


def kernel(
    n_tm, n_h, n_w, scale,
    video, out_grad, lengths_in, t_weight_in, s_weight_in,
    video_grad, t_out, s_out,
    clip, grads, act, act_got, act_sent, delta, delta_got, delta_sent,
    slope, act_grad, moved, plane, wide, s_total, t_total, s_bufs, t_bufs,
    t_fwd, t_bwd, s_fwd, s_bwd, lengths, t_weight, s_weight,
    local_sem, vz_send, vz_recv, vh_send, vh_recv, a_send, a_recv, d_send, d_recv, o_send, o_recv, s_sems, t_sems,
):
    tm = lax.axis_index("tm")
    h = lax.axis_index("height")
    w = lax.axis_index("width")
    frames, cols, rows, chans = delta.shape
    pair = frames // n_tm
    up, down = (h + n_h - 1) % n_h, (h + 1) % n_h
    block = w * n_tm + tm
    blocks = n_w * n_tm
    left, right = (block + blocks - 1) % blocks, (block + 1) % blocks
    left_tm, left_w = left % n_tm, left // n_tm
    right_tm, right_w = right % n_tm, right // n_tm
    around = (
        (tm, up, w), (tm, down, w), (left_tm, h, left_w), (right_tm, h, right_w),
        (left_tm, up, left_w), (left_tm, down, left_w), (right_tm, up, right_w), (right_tm, down, right_w),
    )

    loads = [
        pltpu.make_async_copy(src, dst, local_sem.at[i])
        for i, (src, dst) in enumerate(((t_weight_in, t_weight), (s_weight_in, s_weight), (lengths_in, lengths)))
    ]
    for load in loads:
        load.start()
    barrier = pltpu.get_barrier_semaphore()

    def greet_h(d, carry):
        pl.semaphore_signal(barrier, inc=1, device_id=(tm, (h + d) % n_h, w), device_id_type=MESH)
        return carry

    def greet_z(d, carry):
        pl.semaphore_signal(barrier, inc=1, device_id=((tm + d) % n_tm, h, w), device_id_type=MESH)
        return carry

    lax.fori_loop(1, n_tm, greet_z, 0)
    lax.fori_loop(1, n_h, greet_h, 0)
    pl.semaphore_signal(barrier, inc=1, device_id=(tm, h, 1 - w), device_id_type=MESH)
    for other in around[2:]:
        pl.semaphore_signal(barrier, inc=1, device_id=other, device_id_type=MESH)
    pl.semaphore_wait(barrier, n_tm - 1 + n_h - 1 + 1 + 6)

    def vz_copy(d):
        to = (tm + d) % n_tm
        return pltpu.make_async_remote_copy(
            src_ref=out_grad.at[0, pl.ds(to * cols, cols)], dst_ref=grads.at[tm],
            send_sem=vz_send.at[d], recv_sem=vz_recv.at[d], device_id=(to, h, w), device_id_type=MESH)

    def vh_copy(d):
        to = (h + d) % n_h
        return pltpu.make_async_remote_copy(
            src_ref=video.at[0, 0, :, pl.ds(pl.multiple_of(to * rows, rows), rows)], dst_ref=clip.at[h, pl.ds(2, frames)],
            send_sem=vh_send.at[d], recv_sem=vh_recv.at[d], device_id=(tm, to, w), device_id_type=MESH)

    def step_of(j):
        return (((j + 1) // 2) * (2 * (j % 2) - 1) + n_tm) % n_tm

    lax.fori_loop(1, n_h, started(vh_copy), 0)
    lax.fori_loop(1, n_tm, lambda j, carry: started(vz_copy)(step_of(j), carry), 0)
    own_grad = pltpu.make_async_copy(out_grad.at[0, pl.ds(tm * cols, cols)], grads.at[tm], local_sem.at[3])
    own_clip = pltpu.make_async_copy(
        video.at[0, 0, :, pl.ds(pl.multiple_of(h * rows, rows), rows)], clip.at[h, pl.ds(2, frames)], local_sem.at[4])
    own_grad.start()
    own_clip.start()

    for f in range(2):
        clip[:, f] = jnp.zeros((cols, rows, chans), BF16)
        act_grad[frames + f] = jnp.zeros((cols * rows, chans), BF16)
    for load in loads:
        load.wait()
    for k in range(3):
        t_fwd[k * chans : (k + 1) * chans, :] = t_weight[k]
        t_bwd[k * chans : (k + 1) * chans, :] = t_weight[k].T
    for b in range(3):
        for a in range(3):
            place = pl.ds((b * 3 + a) * chans, chans)
            s_fwd[place, :] = s_weight[a, b]
            s_bwd[place, :] = s_weight[a, b].T
    s_total[...] = jnp.zeros_like(s_total)
    t_total[...] = jnp.zeros_like(t_total)
    delta_sent[1][...] = jnp.zeros_like(delta_sent[1])
    starts = [lengths[0], lengths[0] + lengths[1], lengths[0] + lengths[1] + lengths[2]]

    def mask(f, lag):
        keep = jnp.where(f >= lag, 1, 0)
        for start in starts:
            keep = jnp.where((start > f - lag) & (start <= f), 0, keep)
        return jnp.broadcast_to(keep.astype(F32), (rows, chans)).astype(BF16)[None]

    own_clip.wait()
    lax.fori_loop(1, n_h, waited(vh_copy), 0)

    def edges_of(value, sent, corner_at, f, i):
        edge, corner = sent
        plane[i] = value.astype(F32)
        edge[0, f] = plane[i, pl.ds(0, cols, stride=rows), :].astype(BF16)
        edge[1, f] = plane[i, pl.ds(rows - 1, cols, stride=rows), :].astype(BF16)
        for k, place in enumerate((0, rows - 1, (cols - 1) * rows, cols * rows - 1)):
            corner[corner_at(k)] = plane[i, place : place + 1, :]

    def act_corner(f):
        return lambda k: (k, pl.ds(f, 1))

    def delta_corner(t, i):
        return lambda k: (k, t, pl.ds(i, 1))

    def flat(blocks):
        return [block.reshape(cols * rows, chans) for block in blocks]

    def act_pair(t, carry):
        lines = []
        for i in range(pair):
            f = t * pair + i
            lines.append(jnp.concatenate(flat([clip[:, f + 2], clip[:, f + 1] * mask(f, 1), clip[:, f] * mask(f, 2)]), axis=1))
        both = jnp.dot(jnp.concatenate(lines, axis=0), t_fwd[...], preferred_element_type=F32).astype(BF16)
        for i in range(pair):
            value = both[i * cols * rows : (i + 1) * cols * rows]
            act[t * pair + i, 1 : cols + 1, :, chans : 2 * chans] = value.reshape(cols, rows, chans)
            edges_of(value, act_sent, act_corner(t * pair + i), t * pair + i, i)
        return carry

    lax.fori_loop(0, n_tm, act_pair, 0)

    def halo_copies(sent, got, first, last, span, part, send, recv):
        (edge, corner), (got_rows, got_cols, got_corner) = sent, got
        parts = [
            (edge.at[0, span], got_rows.at[1, span]), (edge.at[1, span], got_rows.at[0, span]),
            (first, got_cols.at[1, span]), (last, got_cols.at[0, span]),
        ] + [(corner.at[(k, *part)], got_corner.at[(3 - k, *part)]) for k in range(4)]
        return [
            pltpu.make_async_remote_copy(
                src_ref=src, dst_ref=dst, send_sem=send.at[i], recv_sem=recv.at[i], device_id=around[i], device_id_type=MESH)
            for i, (src, dst) in enumerate(parts)
        ]

    mid = pl.ds(chans, chans)
    act_halo = halo_copies(
        act_sent, act_got, act.at[:, 1, :, mid], act.at[:, cols, :, mid], pl.ds(0, frames), (), a_send, a_recv)
    for copy in act_halo:
        copy.start()

    row = lax.broadcasted_iota(jnp.int32, (rows, chans), 0)
    is_first, is_last = row == 0, row == rows - 1
    has_up, has_down = h > 0, h < n_h - 1
    has_side = (block > 0, block < blocks - 1)

    def kept(flag, value):
        return jnp.where(flag, value, jnp.zeros_like(value))

    def shifted(middle, above, below):
        before = jnp.where(is_first, jnp.broadcast_to(above, middle.shape), pltpu.roll(middle, 1, 0))
        after = jnp.where(is_last, jnp.broadcast_to(below, middle.shape), pltpu.roll(middle, rows - 1, 0))
        return before.astype(BF16), after.astype(BF16)

    def with_halo(f, middle_of, got, corner_at, put):
        got_rows, got_cols, got_corner = got
        above = kept(has_up, got_rows[0, f].astype(F32))
        below = kept(has_down, got_rows[1, f].astype(F32))
        for c in range(cols):
            middle = middle_of(c)
            before, after = shifted(middle.astype(F32), above[c : c + 1], below[c : c + 1])
            put(c + 1, before, middle, after)
        for side, c in ((0, 0), (1, cols + 1)):
            middle = kept(has_side[side], got_cols[side, f].astype(F32))
            above_side = kept(has_side[side] & has_up, got_corner[corner_at(2 * side)])
            below_side = kept(has_side[side] & has_down, got_corner[corner_at(2 * side + 1)])
            before, after = shifted(middle, above_side, below_side)
            put(c, before, middle.astype(BF16), after)

    for copy in act_halo:
        copy.wait()

    def slope_pair(t, carry):
        lines = []
        for i in range(pair):
            f = t * pair + i

            def put(c, before, middle, after):
                act[f, c, :, 0:chans] = before
                if c == 0 or c == cols + 1:
                    act[f, c, :, chans : 2 * chans] = middle
                act[f, c, :, 2 * chans : 3 * chans] = after

            with_halo(f, lambda c: act[f, c + 1, :, chans : 2 * chans], act_got, act_corner(f), put)
            lines.append(
                jnp.concatenate([act[f, b : b + cols].reshape(cols * rows, 3 * chans) for b in range(3)], axis=1))
        pre = jnp.dot(jnp.concatenate(lines, axis=0), s_fwd[...], preferred_element_type=F32)
        sig = jax.nn.sigmoid(pre)
        slope[pl.ds(t * pair, pair)] = (sig * (1.0 + pre * (1.0 - sig))).reshape(pair, cols * rows, chans)
        return carry

    lax.fori_loop(0, n_tm, slope_pair, 0)

    def delta_halo(t):
        span = pl.ds(t * pair, pair)
        return halo_copies(
            delta_sent, delta_got, delta.at[span, 0], delta.at[span, cols - 1], span, (t,), d_send.at[t], d_recv.at[t])

    own_grad.wait()

    def delta_pair(j, carry):
        d = step_of(j)
        t = (tm + n_tm - d) % n_tm

        @pl.when(j > 0)
        def _():
            vz_copy(d).wait()

        for i in range(pair):
            f = t * pair + i
            value = (grads[t, :, i].reshape(cols * rows, chans).astype(F32) * slope[f]).astype(BF16)
            delta[f] = value.reshape(cols, rows, chans)
            edges_of(value, delta_sent, delta_corner(t, i), f, i)
        for copy in delta_halo(t):
            copy.start()
        return carry

    def spatial_pair(t, carry):
        span = pl.ds(t * pair, pair)
        here = delta[span].reshape(pair * cols * rows, chans)
        for b in range(3):
            source = act[span, b : b + cols].reshape(pair * cols * rows, 3 * chans)
            s_total[:, b * 3 * chans : (b + 1) * 3 * chans] += lax.dot_general(
                here, source, (((0,), (0,)), ((), ())), preferred_element_type=F32)
        return carry

    def back_pair(t):
        for copy in delta_halo(t):
            copy.wait()
        lines = []
        for i in range(pair):
            f = t * pair + i

            def put(c, before, middle, after):
                wide[i, c, :, 0:chans] = after
                wide[i, c, :, chans : 2 * chans] = middle
                wide[i, c, :, 2 * chans : 3 * chans] = before

            with_halo(f, lambda c: delta[f, c], delta_got, delta_corner(t, i), put)
            lines.append(jnp.concatenate(
                [wide[i, 2 - b : 2 - b + cols].reshape(cols * rows, 3 * chans) for b in range(3)], axis=1))
        value = jnp.dot(jnp.concatenate(lines, axis=0), s_bwd[...], preferred_element_type=F32).astype(BF16)
        act_grad[pl.ds(t * pair, pair)] = value.reshape(pair, cols * rows, chans)

    lax.fori_loop(0, n_tm, delta_pair, 0)
    lax.fori_loop(0, n_tm, spatial_pair, 0)

    def device(t, row_band, core):
        return {"device_id": (t, row_band, core), "device_id_type": MESH}

    def summed_over_all(terms, out, bufs, sems):
        pair_buf, half, h_buf, z_buf, got_mine, got_theirs = bufs
        swap_sem, h_send, h_recv, z_send, z_recv, g_send, g_recv, f_sem = sems
        taps = half.shape[0]
        piece = chans // n_h
        mine, theirs = pl.ds(w * taps, taps), pl.ds((1 - w) * taps, taps)

        def band(i):
            return pl.ds(pl.multiple_of(i * piece, piece), piece)

        swap = pltpu.make_async_remote_copy(
            src_ref=terms.at[theirs], dst_ref=pair_buf, send_sem=swap_sem.at[0], recv_sem=swap_sem.at[1],
            **device(tm, h, 1 - w))

        def h_copy(d):
            to = (h + d) % n_h
            return pltpu.make_async_remote_copy(
                src_ref=half.at[:, band(to)], dst_ref=h_buf.at[d], send_sem=h_send.at[d], recv_sem=h_recv.at[d],
                **device(tm, to, w))

        def z_copy(d):
            return pltpu.make_async_remote_copy(
                src_ref=z_buf.at[tm], dst_ref=z_buf.at[tm], send_sem=z_send.at[d], recv_sem=z_recv.at[d],
                **device((tm + d) % n_tm, h, w))

        def g_copy(d):
            return pltpu.make_async_remote_copy(
                src_ref=got_mine.at[h], dst_ref=got_mine.at[h], send_sem=g_send.at[d], recv_sem=g_recv.at[d],
                **device(tm, (h + d) % n_h, w))

        share = pltpu.make_async_remote_copy(
            src_ref=got_mine, dst_ref=got_theirs, send_sem=f_sem.at[0], recv_sem=f_sem.at[1],
            **device(tm, h, 1 - w))

        def stage0():
            swap.start()

        def stage1():
            swap.wait()
            half[...] = terms[mine] + pair_buf[...]
            lax.fori_loop(1, n_h, started(h_copy), 0)

        def stage2():
            lax.fori_loop(1, n_h, waited(h_copy), 0)
            total = half[:, band(h), :]
            for d in range(1, n_h):
                total = total + h_buf[d]
            z_buf[tm] = total
            lax.fori_loop(1, n_tm, started(z_copy), 0)

        def stage3():
            lax.fori_loop(1, n_tm, waited(z_copy), 0)
            total = z_buf[0]
            for t in range(1, n_tm):
                total = total + z_buf[t]
            got_mine[h] = total.astype(BF16)
            lax.fori_loop(1, n_h, started(g_copy), 0)

        def stage4():
            lax.fori_loop(1, n_h, waited(g_copy), 0)
            share.start()
            for i in range(n_h):
                out[mine, i * piece : (i + 1) * piece, :] = got_mine[i].astype(F32)

        def stage5():
            share.wait()
            for i in range(n_h):
                out[theirs, i * piece : (i + 1) * piece, :] = got_theirs[i].astype(F32)

        return stage0, stage1, stage2, stage3, stage4, stage5

    s_terms, t_terms = s_bufs[0], t_bufs[0]
    s_stage = summed_over_all(s_terms, s_out, s_bufs[1:], s_sems)
    t_stage = summed_over_all(t_terms, t_out, t_bufs[1:], t_sems)
    for a in range(3):
        for b in range(3):
            s_terms[a * 3 + b] = s_total[:, (b * 3 + a) * chans : (b * 3 + a + 1) * chans].T * scale
    for k in range(9, s_terms.shape[0]):
        s_terms[k] = jnp.zeros((chans, chans), F32)
    s_stage[0]()

    def parts_of(t):
        lines = []
        for i in range(pair):
            f = t * pair + i
            lines.append(jnp.concatenate([
                act_grad[f],
                (act_grad[f + 1].reshape(cols, rows, chans) * mask(f + 1, 1)).reshape(cols * rows, chans),
                (act_grad[f + 2].reshape(cols, rows, chans) * mask(f + 2, 2)).reshape(cols * rows, chans),
            ], axis=1))
        return lines

    def time_pair(t):
        here = jnp.concatenate(flat([clip[:, t * pair + 2 + i] for i in range(pair)]), axis=0)
        parts = jnp.concatenate(parts_of(t), axis=0)
        t_total[...] += lax.dot_general(here, parts, (((0,), (0,)), ((), ())), preferred_element_type=F32)
        value = jnp.dot(parts, t_bwd[...], preferred_element_type=F32).astype(BF16)
        for i in range(pair):
            moved[:, t * pair + i] = value[i * cols * rows : (i + 1) * cols * rows].reshape(cols, rows, chans)

    def back_time(t, carry):
        back_pair(t)

        @pl.when(t >= 1)
        def _():
            time_pair(t - 1)

        return carry

    chunks = o_send.shape[0]
    length = frames // chunks

    def out_place(i):
        return video_grad.at[0, 0, pl.ds(i * length, length), pl.ds(pl.multiple_of(h * rows, rows), rows)]

    def out_copy(i):
        def copy(d):
            to = (h + d) % n_h
            return pltpu.make_async_remote_copy(
                src_ref=moved.at[to, pl.ds(i * length, length)], dst_ref=out_place(i),
                send_sem=o_send.at[i, d], recv_sem=o_recv.at[i, d], **device(tm, to, w))

        return copy

    def own_out(i):
        return pltpu.make_async_copy(moved.at[h, pl.ds(i * length, length)], out_place(i), local_sem.at[5 + i])

    def send_back(i):
        lax.fori_loop(1, n_h, started(out_copy(i)), 0)
        own_out(i).start()

    after = {0: s_stage[1], 2: s_stage[2]}
    per = n_tm // chunks
    for i in range(chunks):
        lax.fori_loop(i * per + (i > 0), min((i + 1) * per + 1, n_tm), back_time, 0)
        if i in after:
            after[i]()
        if i < chunks - 1:
            send_back(i)
    time_pair(n_tm - 1)
    for k in range(3):
        t_terms[k] = t_total[:, k * chans : (k + 1) * chans] * scale
    for k in range(3, t_terms.shape[0]):
        t_terms[k] = jnp.zeros((chans, chans), F32)
    t_stage[0]()
    t_stage[1]()
    t_stage[2]()
    send_back(chunks - 1)
    s_stage[3]()
    t_stage[3]()
    s_stage[4]()
    t_stage[4]()
    s_stage[5]()
    for i in range(chunks):
        own_out(i).wait()
        lax.fori_loop(1, n_h, waited(out_copy(i)), 0)
    t_stage[5]()


def shards(n_tm, n_h, n_w, video, out_grad, lengths, temporal_weight, spatial_weight):
    frames, all_rows, chans = video.shape[2:]
    rows = all_rows // n_h
    cols = out_grad.shape[1] // n_tm
    pair = frames // n_tm
    lags = temporal_weight.shape[0]
    offs = spatial_weight.shape[0]
    s_taps = -(-offs * offs // n_w)
    t_taps = -(-lags // n_w)
    chunks = 4
    scale = float(frames * all_rows * cols * n_tm * n_w) ** (-0.5)
    dma = pltpu.SemaphoreType.DMA
    vmem = pltpu.VMEM

    def sum_bufs(taps):
        return [
            vmem((n_w * taps, chans, chans), F32),
            vmem((taps, chans, chans), F32),
            vmem((taps, chans, chans), F32),
            vmem((n_h, taps, chans // n_h, chans), F32),
            vmem((n_tm, taps, chans // n_h, chans), F32),
            vmem((n_h, taps, chans // n_h, chans), BF16),
            vmem((n_h, taps, chans // n_h, chans), BF16),
        ]

    def sum_sems():
        return [dma((2,)), dma((n_h,)), dma((n_h,)), dma((n_tm,)), dma((n_tm,)), dma((n_h,)), dma((n_h,)), dma((2,))]

    hbm = pl.BlockSpec(memory_space=pltpu.HBM)
    video_grad, t_sum, s_sum = pl.pallas_call(
        functools.partial(kernel, n_tm, n_h, n_w, scale),
        out_shape=(
            jax.ShapeDtypeStruct(video.shape, BF16),
            jax.ShapeDtypeStruct((n_w * t_taps, chans, chans), F32),
            jax.ShapeDtypeStruct((n_w * s_taps, chans, chans), F32),
        ),
        in_specs=[hbm] * 5,
        out_specs=(
            pl.BlockSpec(memory_space=pl.ANY), pl.BlockSpec(memory_space=pltpu.VMEM), pl.BlockSpec(memory_space=pltpu.VMEM)),
        scratch_shapes=[
            vmem((cols, frames + 2, rows, chans), BF16),
            vmem((n_tm, cols, pair, rows, chans), BF16),
            vmem((frames, cols + 2, rows, 3 * chans), BF16),
            [vmem((2, frames, cols, chans), BF16), vmem((2, frames, rows, chans), BF16), vmem((4, frames, chans), F32)],
            [vmem((2, frames, cols, chans), BF16), vmem((4, frames, chans), F32)],
            vmem((frames, cols, rows, chans), BF16),
            [vmem((2, frames, cols, chans), BF16), vmem((2, frames, rows, chans), BF16), vmem((4, n_tm, 8, chans), F32)],
            [vmem((2, frames, cols, chans), BF16), vmem((4, n_tm, 8, chans), F32)],
            vmem((frames, cols * rows, chans), F32),
            vmem((frames + 2, cols * rows, chans), BF16),
            vmem((cols, frames, rows, chans), BF16),
            vmem((pair, cols * rows, chans), F32),
            vmem((pair, cols + 2, rows, 3 * chans), BF16),
            vmem((chans, offs * offs * chans), F32),
            vmem((chans, lags * chans), F32),
            sum_bufs(s_taps),
            sum_bufs(t_taps),
            vmem((lags * chans, chans), BF16),
            vmem((lags * chans, chans), BF16),
            vmem((offs * offs * chans, chans), BF16),
            vmem((offs * offs * chans, chans), BF16),
            pltpu.SMEM(lengths.shape, jnp.int32),
            vmem(temporal_weight.shape, BF16),
            vmem(spatial_weight.shape, BF16),
            dma((5 + chunks,)), dma((n_tm,)), dma((n_tm,)), dma((n_h,)), dma((n_h,)), dma((8,)), dma((8,)),
            dma((n_tm, 8)), dma((n_tm, 8)), dma((chunks, n_h)), dma((chunks, n_h)),
            sum_sems(),
            sum_sems(),
        ],
        compiler_params=pltpu.CompilerParams(collective_id=0, has_side_effects=True, vmem_limit_bytes=54 << 20),
    )(video, out_grad, lengths, temporal_weight, spatial_weight)
    return (
        video_grad,
        t_sum[:lags],
        s_sum[: offs * offs].reshape(offs, offs, chans, chans),
    )


def solution(mesh):
    placed = (
        P("width", ("tm", "height"), None, None, None),
        P("width", None, "tm", "height", None),
        P(),
        P(),
        P(),
    )
    return jax.shard_map(
        functools.partial(shards, mesh.shape["tm"], mesh.shape["height"], mesh.shape["width"]),
        mesh=mesh,
        in_specs=placed,
        out_specs=(P("width", ("tm", "height"), None, None, None), P(), P()),
        check_vma=False,
    )
```

```python
import functools

import jax
import jax.numpy as jnp
from jax import lax
from jax.experimental import pallas as pl
from jax.experimental.pallas import tpu as pltpu
from jax.sharding import PartitionSpec as P

MESH = pl.DeviceIdType.MESH
BF16 = jnp.bfloat16
F32 = jnp.float32


def started(copy):
    def body(d, carry):
        copy(d).start()
        return carry

    return body


def waited(copy):
    def body(d, carry):
        copy(d).wait()
        return carry

    return body


def kernel(
    n_tm, n_h, n_w, scale,
    video, out_grad, lengths_in, t_weight_in, s_weight_in,
    video_grad, t_sum, s_sum,
    clip, grads, act, act_side, act_got, act_sent, delta, delta_got, delta_sent,
    slope, act_grad, moved, plane, wide, s_total, t_total, s_bufs, t_bufs, s_out, t_out,
    t_fwd, t_bwd, s_fwd, s_bwd, lengths, t_weight, s_weight,
    local_sem, vz_send, vz_recv, vh_send, vh_recv, a_send, a_recv, d_send, d_recv, o_send, o_recv, s_sems, t_sems,
):
    tm = lax.axis_index("tm")
    h = lax.axis_index("height")
    w = lax.axis_index("width")
    frames, cols, rows, chans = delta.shape
    pair = frames // n_tm
    up, down = (h + n_h - 1) % n_h, (h + 1) % n_h
    block = w * n_tm + tm
    blocks = n_w * n_tm
    left, right = (block + blocks - 1) % blocks, (block + 1) % blocks
    left_tm, left_w = left % n_tm, left // n_tm
    right_tm, right_w = right % n_tm, right // n_tm
    around = (
        (tm, up, w), (tm, down, w), (left_tm, h, left_w), (right_tm, h, right_w),
        (left_tm, up, left_w), (left_tm, down, left_w), (right_tm, up, right_w), (right_tm, down, right_w),
    )

    loads = [
        pltpu.make_async_copy(src, dst, local_sem.at[i])
        for i, (src, dst) in enumerate(((t_weight_in, t_weight), (s_weight_in, s_weight), (lengths_in, lengths)))
    ]
    for load in loads:
        load.start()
    barrier = pltpu.get_barrier_semaphore()

    def greet_h(d, carry):
        pl.semaphore_signal(barrier, inc=1, device_id=(tm, (h + d) % n_h, w), device_id_type=MESH)
        return carry

    def greet_z(d, carry):
        pl.semaphore_signal(barrier, inc=1, device_id=((tm + d) % n_tm, h, w), device_id_type=MESH)
        return carry

    lax.fori_loop(1, n_tm, greet_z, 0)
    lax.fori_loop(1, n_h, greet_h, 0)
    pl.semaphore_signal(barrier, inc=1, device_id=(tm, h, 1 - w), device_id_type=MESH)
    for other in around[2:]:
        pl.semaphore_signal(barrier, inc=1, device_id=other, device_id_type=MESH)
    pl.semaphore_wait(barrier, n_tm - 1 + n_h - 1 + 1 + 6)

    def vz_copy(d):
        to = (tm + d) % n_tm
        return pltpu.make_async_remote_copy(
            src_ref=out_grad.at[0, pl.ds(to * cols, cols)], dst_ref=grads.at[tm],
            send_sem=vz_send.at[d], recv_sem=vz_recv.at[d], device_id=(to, h, w), device_id_type=MESH)

    parts_in = vh_send.shape[0]
    run = frames // parts_in

    def vh_copy(i):
        def copy(d):
            to = (h + d) % n_h
            return pltpu.make_async_remote_copy(
                src_ref=video.at[0, 0, pl.ds(i * run, run), pl.ds(pl.multiple_of(to * rows, rows), rows)],
                dst_ref=clip.at[h, pl.ds(2 + i * run, run)],
                send_sem=vh_send.at[i, d], recv_sem=vh_recv.at[i, d], device_id=(tm, to, w), device_id_type=MESH)

        return copy

    def step_of(j):
        return (((j + 1) // 2) * (2 * (j % 2) - 1) + n_tm) % n_tm

    for i in range(parts_in):
        lax.fori_loop(1, n_h, started(vh_copy(i)), 0)
    lax.fori_loop(1, n_tm, lambda j, carry: started(vz_copy)(step_of(j), carry), 0)
    own_grad = pltpu.make_async_copy(out_grad.at[0, pl.ds(tm * cols, cols)], grads.at[tm], local_sem.at[3])
    own_clip = pltpu.make_async_copy(
        video.at[0, 0, :, pl.ds(pl.multiple_of(h * rows, rows), rows)], clip.at[h, pl.ds(2, frames)], local_sem.at[4])
    own_grad.start()
    own_clip.start()

    for f in range(2):
        clip[:, f] = jnp.zeros((cols, rows, chans), BF16)
        act_grad[frames + f] = jnp.zeros((cols * rows, chans), BF16)
    for load in loads:
        load.wait()
    for k in range(3):
        t_fwd[k * chans : (k + 1) * chans, :] = t_weight[k]
        t_bwd[k * chans : (k + 1) * chans, :] = t_weight[k].T
    for b in range(3):
        for a in range(3):
            place = pl.ds((b * 3 + a) * chans, chans)
            s_fwd[place, :] = s_weight[a, b]
            s_bwd[place, :] = s_weight[a, b].T
    s_total[...] = jnp.zeros_like(s_total)
    t_total[...] = jnp.zeros_like(t_total)
    delta_sent[1][...] = jnp.zeros_like(delta_sent[1])
    starts = [lengths[0], lengths[0] + lengths[1], lengths[0] + lengths[1] + lengths[2]]

    def mask(f, lag):
        keep = jnp.where(f >= lag, 1, 0)
        for start in starts:
            keep = jnp.where((start > f - lag) & (start <= f), 0, keep)
        return jnp.broadcast_to(keep.astype(F32), (rows, chans)).astype(BF16)[None]

    own_clip.wait()

    def edges_of(value, sent, corner_at, f, i):
        edge, corner = sent
        plane[i] = value.astype(F32)
        edge[0, f] = plane[i, pl.ds(0, cols, stride=rows), :].astype(BF16)
        edge[1, f] = plane[i, pl.ds(rows - 1, cols, stride=rows), :].astype(BF16)
        for k, place in enumerate((0, rows - 1, (cols - 1) * rows, cols * rows - 1)):
            corner[corner_at(k)] = plane[i, place : place + 1, :]

    def act_corner(f):
        return lambda k: (k, pl.ds(f, 1))

    def delta_corner(t, i):
        return lambda k: (k, t, pl.ds(i, 1))

    def flat(blocks):
        return [block.reshape(cols * rows, chans) for block in blocks]

    def act_pair(t, carry):
        lines = []
        for i in range(pair):
            f = t * pair + i
            lines.append(jnp.concatenate(flat([clip[:, f + 2], clip[:, f + 1] * mask(f, 1), clip[:, f] * mask(f, 2)]), axis=1))
        both = jnp.dot(jnp.concatenate(lines, axis=0), t_fwd[...], preferred_element_type=F32).astype(BF16)
        for i in range(pair):
            value = both[i * cols * rows : (i + 1) * cols * rows]
            act[t * pair + i, 1 : cols + 1, :, chans : 2 * chans] = value.reshape(cols, rows, chans)
            act_side[0, t * pair + i] = value[:rows]
            act_side[1, t * pair + i] = value[(cols - 1) * rows :]
            edges_of(value, act_sent, act_corner(t * pair + i), t * pair + i, i)
        return carry

    def halo_copies(sent, got, first, last, span, part, send, recv):
        (edge, corner), (got_rows, got_cols, got_corner) = sent, got
        parts = [
            (edge.at[0, span], got_rows.at[1, span]), (edge.at[1, span], got_rows.at[0, span]),
            (first, got_cols.at[1, span]), (last, got_cols.at[0, span]),
        ] + [(corner.at[(k, *part)], got_corner.at[(3 - k, *part)]) for k in range(4)]
        return [
            pltpu.make_async_remote_copy(
                src_ref=src, dst_ref=dst, send_sem=send.at[i], recv_sem=recv.at[i], device_id=around[i], device_id_type=MESH)
            for i, (src, dst) in enumerate(parts)
        ]

    def act_halo(i):
        span = pl.ds(i * run, run)
        return halo_copies(
            act_sent, act_got, act_side.at[0, span], act_side.at[1, span], span, (span,), a_send.at[i], a_recv.at[i])

    for i in range(parts_in):
        lax.fori_loop(1, n_h, waited(vh_copy(i)), 0)
        lax.fori_loop(i * run // pair, (i + 1) * run // pair, act_pair, 0)
        for copy in act_halo(i):
            copy.start()

    row = lax.broadcasted_iota(jnp.int32, (rows, chans), 0)
    is_first, is_last = row == 0, row == rows - 1
    has_up, has_down = h > 0, h < n_h - 1
    has_side = (block > 0, block < blocks - 1)

    def kept(flag, value):
        return jnp.where(flag, value, jnp.zeros_like(value))

    def shifted(middle, above, below):
        before = jnp.where(is_first, jnp.broadcast_to(above, middle.shape), pltpu.roll(middle, 1, 0))
        after = jnp.where(is_last, jnp.broadcast_to(below, middle.shape), pltpu.roll(middle, rows - 1, 0))
        return before.astype(BF16), after.astype(BF16)

    def with_halo(f, middle_of, got, corner_at, put):
        got_rows, got_cols, got_corner = got
        above = kept(has_up, got_rows[0, f].astype(F32))
        below = kept(has_down, got_rows[1, f].astype(F32))
        for c in range(cols):
            middle = middle_of(c)
            before, after = shifted(middle.astype(F32), above[c : c + 1], below[c : c + 1])
            put(c + 1, before, middle, after)
        for side, c in ((0, 0), (1, cols + 1)):
            middle = kept(has_side[side], got_cols[side, f].astype(F32))
            above_side = kept(has_side[side] & has_up, got_corner[corner_at(2 * side)])
            below_side = kept(has_side[side] & has_down, got_corner[corner_at(2 * side + 1)])
            before, after = shifted(middle, above_side, below_side)
            put(c, before, middle.astype(BF16), after)


    def slope_pair(t, carry):
        lines = []
        for i in range(pair):
            f = t * pair + i

            def put(c, before, middle, after):
                act[f, c, :, 0:chans] = before
                if c == 0 or c == cols + 1:
                    act[f, c, :, chans : 2 * chans] = middle
                act[f, c, :, 2 * chans : 3 * chans] = after

            with_halo(f, lambda c: act[f, c + 1, :, chans : 2 * chans], act_got, act_corner(f), put)
            lines.append(
                jnp.concatenate([act[f, b : b + cols].reshape(cols * rows, 3 * chans) for b in range(3)], axis=1))
        pre = jnp.dot(jnp.concatenate(lines, axis=0), s_fwd[...], preferred_element_type=F32)
        sig = jax.nn.sigmoid(pre)
        slope[pl.ds(t * pair, pair)] = (sig * (1.0 + pre * (1.0 - sig))).reshape(pair, cols * rows, chans)
        return carry

    for i in range(parts_in):
        for copy in act_halo(i):
            copy.wait()
        lax.fori_loop(i * run // pair, (i + 1) * run // pair, slope_pair, 0)

    def delta_halo(t):
        span = pl.ds(t * pair, pair)
        return halo_copies(
            delta_sent, delta_got, delta.at[span, 0], delta.at[span, cols - 1], span, (t,), d_send.at[t], d_recv.at[t])

    own_grad.wait()

    def delta_pair(j, carry):
        d = step_of(j)
        t = (tm + n_tm - d) % n_tm

        @pl.when(j > 0)
        def _():
            vz_copy(d).wait()

        for i in range(pair):
            f = t * pair + i
            value = (grads[t, :, i].reshape(cols * rows, chans).astype(F32) * slope[f]).astype(BF16)
            delta[f] = value.reshape(cols, rows, chans)
            edges_of(value, delta_sent, delta_corner(t, i), f, i)
        for copy in delta_halo(t):
            copy.start()
        return carry

    def spatial_part(t, carry):
        span = pl.ds(t * 2 * pair, 2 * pair)
        here = delta[span].reshape(2 * pair * cols * rows, chans)
        for b in range(3):
            source = act[span, b : b + cols].reshape(2 * pair * cols * rows, 3 * chans)
            s_total[:, b * 3 * chans : (b + 1) * 3 * chans] += lax.dot_general(
                here, source, (((0,), (0,)), ((), ())), preferred_element_type=F32)
        return carry

    def back_pair(t):
        for copy in delta_halo(t):
            copy.wait()
        lines = []
        for i in range(pair):
            f = t * pair + i

            def put(c, before, middle, after):
                wide[i, c, :, 0:chans] = after
                wide[i, c, :, chans : 2 * chans] = middle
                wide[i, c, :, 2 * chans : 3 * chans] = before

            with_halo(f, lambda c: delta[f, c], delta_got, delta_corner(t, i), put)
            lines.append(jnp.concatenate(
                [wide[i, 2 - b : 2 - b + cols].reshape(cols * rows, 3 * chans) for b in range(3)], axis=1))
        value = jnp.dot(jnp.concatenate(lines, axis=0), s_bwd[...], preferred_element_type=F32).astype(BF16)
        act_grad[pl.ds(t * pair, pair)] = value.reshape(pair, cols * rows, chans)

    lax.fori_loop(0, n_tm, delta_pair, 0)
    lax.fori_loop(0, n_tm // 2, spatial_part, 0)

    def device(t, row_band, core):
        return {"device_id": (t, row_band, core), "device_id_type": MESH}

    def summed_over_all(terms, out, bufs, sems):
        pair_buf, half, h_buf, z_buf, got_mine, got_theirs = bufs
        swap_sem, h_send, h_recv, z_send, z_recv, g_send, g_recv, f_sem = sems
        taps = half.shape[0]
        piece = chans // n_h
        mine, theirs = pl.ds(w * taps, taps), pl.ds((1 - w) * taps, taps)

        def band(i):
            return pl.ds(pl.multiple_of(i * piece, piece), piece)

        swap = pltpu.make_async_remote_copy(
            src_ref=terms.at[theirs], dst_ref=pair_buf, send_sem=swap_sem.at[0], recv_sem=swap_sem.at[1],
            **device(tm, h, 1 - w))

        def h_copy(d):
            to = (h + d) % n_h
            return pltpu.make_async_remote_copy(
                src_ref=half.at[:, band(to)], dst_ref=h_buf.at[d], send_sem=h_send.at[d], recv_sem=h_recv.at[d],
                **device(tm, to, w))

        def z_copy(d):
            return pltpu.make_async_remote_copy(
                src_ref=z_buf.at[tm], dst_ref=z_buf.at[tm], send_sem=z_send.at[d], recv_sem=z_recv.at[d],
                **device((tm + d) % n_tm, h, w))

        def g_copy(d):
            return pltpu.make_async_remote_copy(
                src_ref=got_mine.at[h], dst_ref=got_mine.at[h], send_sem=g_send.at[d], recv_sem=g_recv.at[d],
                **device(tm, (h + d) % n_h, w))

        share = pltpu.make_async_remote_copy(
            src_ref=got_mine, dst_ref=got_theirs, send_sem=f_sem.at[0], recv_sem=f_sem.at[1],
            **device(tm, h, 1 - w))

        def gather(place, got):
            for i in range(0, n_h, 2):
                both = jnp.concatenate([got[i].astype(F32), got[i + 1].astype(F32)], axis=1)
                out[place, i * piece : (i + 2) * piece, :] = both.astype(BF16)

        def stage0():
            swap.start()

        def stage1():
            swap.wait()
            half[...] = terms[mine] + pair_buf[...]
            lax.fori_loop(1, n_h, started(h_copy), 0)

        def stage2():
            lax.fori_loop(1, n_h, waited(h_copy), 0)
            total = half[:, band(h), :]
            for d in range(1, n_h):
                total = total + h_buf[d]
            z_buf[tm] = total
            lax.fori_loop(1, n_tm, started(z_copy), 0)

        def stage3():
            lax.fori_loop(1, n_tm, waited(z_copy), 0)
            total = z_buf[0]
            for t in range(1, n_tm):
                total = total + z_buf[t]
            got_mine[h] = total.astype(BF16)
            lax.fori_loop(1, n_h, started(g_copy), 0)

        def stage4():
            lax.fori_loop(1, n_h, waited(g_copy), 0)
            share.start()
            gather(mine, got_mine)

        def stage5():
            share.wait()
            gather(theirs, got_theirs)

        return stage0, stage1, stage2, stage3, stage4, stage5

    s_terms, t_terms = s_bufs[0], t_bufs[0]
    s_stage = summed_over_all(s_terms, s_out, s_bufs[1:], s_sems)
    t_stage = summed_over_all(t_terms, t_out, t_bufs[1:], t_sems)
    for a in range(3):
        for b in range(3):
            s_terms[a * 3 + b] = s_total[:, (b * 3 + a) * chans : (b * 3 + a + 1) * chans].T * scale
    for k in range(9, s_terms.shape[0]):
        s_terms[k] = jnp.zeros((chans, chans), F32)
    s_stage[0]()

    def parts_of(t):
        lines = []
        for i in range(pair):
            f = t * pair + i
            lines.append(jnp.concatenate([
                act_grad[f],
                (act_grad[f + 1].reshape(cols, rows, chans) * mask(f + 1, 1)).reshape(cols * rows, chans),
                (act_grad[f + 2].reshape(cols, rows, chans) * mask(f + 2, 2)).reshape(cols * rows, chans),
            ], axis=1))
        return lines

    def weight_pair(t):
        here = jnp.concatenate(flat([clip[:, t * pair + 2 + i] for i in range(pair)]), axis=0)
        parts = jnp.concatenate(parts_of(t), axis=0)
        t_total[...] += lax.dot_general(here, parts, (((0,), (0,)), ((), ())), preferred_element_type=F32)
        return parts

    def video_pair(t, parts):
        value = jnp.dot(parts, t_bwd[...], preferred_element_type=F32).astype(BF16)
        for i in range(pair):
            moved[:, t * pair + i] = value[i * cols * rows : (i + 1) * cols * rows].reshape(cols, rows, chans)

    def back_time(t, carry):
        back_pair(t)

        @pl.when(t >= 1)
        def _():
            video_pair(t - 1, weight_pair(t - 1))

        return carry

    chunks = o_send.shape[0]
    length = frames // chunks

    def out_place(i):
        return video_grad.at[0, 0, pl.ds(i * length, length), pl.ds(pl.multiple_of(h * rows, rows), rows)]

    def out_copy(i):
        def copy(d):
            to = (h + d) % n_h
            return pltpu.make_async_remote_copy(
                src_ref=moved.at[to, pl.ds(i * length, length)], dst_ref=out_place(i),
                send_sem=o_send.at[i, d], recv_sem=o_recv.at[i, d], **device(tm, to, w))

        return copy

    def own_out(i):
        return pltpu.make_async_copy(moved.at[h, pl.ds(i * length, length)], out_place(i), local_sem.at[5 + i])

    def send_back(i):
        lax.fori_loop(1, n_h, started(out_copy(i)), 0)
        own_out(i).start()

    after = {0: s_stage[1], 2: s_stage[2]}
    per = n_tm // chunks
    for i in range(chunks):
        lax.fori_loop(i * per + (i > 0), min((i + 1) * per + 1, n_tm), back_time, 0)
        if i in after:
            after[i]()
        if i < chunks - 1:
            send_back(i)
    last_parts = weight_pair(n_tm - 1)
    for k in range(3):
        t_terms[k] = t_total[:, k * chans : (k + 1) * chans] * scale
    for k in range(3, t_terms.shape[0]):
        t_terms[k] = jnp.zeros((chans, chans), F32)
    t_stage[0]()
    video_pair(n_tm - 1, last_parts)
    t_stage[1]()
    t_stage[2]()
    send_back(chunks - 1)
    s_stage[3]()
    t_stage[3]()
    s_stage[4]()
    t_stage[4]()
    s_stage[5]()
    s_sum[...] = s_out[0 : s_sum.shape[0]]
    for i in range(chunks):
        own_out(i).wait()
        lax.fori_loop(1, n_h, waited(out_copy(i)), 0)
    t_stage[5]()
    t_sum[...] = t_out[0 : t_sum.shape[0]]


def shards(n_tm, n_h, n_w, video, out_grad, lengths, temporal_weight, spatial_weight):
    frames, all_rows, chans = video.shape[2:]
    rows = all_rows // n_h
    cols = out_grad.shape[1] // n_tm
    pair = frames // n_tm
    lags = temporal_weight.shape[0]
    offs = spatial_weight.shape[0]
    s_taps = -(-offs * offs // n_w)
    t_taps = -(-lags // n_w)
    chunks = 4
    scale = float(frames * all_rows * cols * n_tm * n_w) ** (-0.5)
    dma = pltpu.SemaphoreType.DMA
    vmem = pltpu.VMEM

    def sum_bufs(taps):
        return [
            vmem((n_w * taps, chans, chans), F32),
            vmem((taps, chans, chans), F32),
            vmem((taps, chans, chans), F32),
            vmem((n_h, taps, chans // n_h, chans), F32),
            vmem((n_tm, taps, chans // n_h, chans), F32),
            vmem((n_h, taps, chans // n_h, chans), BF16),
            vmem((n_h, taps, chans // n_h, chans), BF16),
        ]

    def sum_sems():
        return [dma((2,)), dma((n_h,)), dma((n_h,)), dma((n_tm,)), dma((n_tm,)), dma((n_h,)), dma((n_h,)), dma((2,))]

    hbm = pl.BlockSpec(memory_space=pltpu.HBM)
    video_grad, t_sum, s_sum = pl.pallas_call(
        functools.partial(kernel, n_tm, n_h, n_w, scale),
        out_shape=(
            jax.ShapeDtypeStruct(video.shape, BF16),
            jax.ShapeDtypeStruct((lags, chans, chans), BF16),
            jax.ShapeDtypeStruct((offs * offs, chans, chans), BF16),
        ),
        in_specs=[hbm] * 5,
        out_specs=(
            pl.BlockSpec(memory_space=pl.ANY), pl.BlockSpec(memory_space=pltpu.VMEM), pl.BlockSpec(memory_space=pltpu.VMEM)),
        scratch_shapes=[
            vmem((cols, frames + 2, rows, chans), BF16),
            vmem((n_tm, cols, pair, rows, chans), BF16),
            vmem((frames, cols + 2, rows, 3 * chans), BF16),
            vmem((2, frames, rows, chans), BF16),
            [vmem((2, frames, cols, chans), BF16), vmem((2, frames, rows, chans), BF16), vmem((4, frames, chans), F32)],
            [vmem((2, frames, cols, chans), BF16), vmem((4, frames, chans), F32)],
            vmem((frames, cols, rows, chans), BF16),
            [vmem((2, frames, cols, chans), BF16), vmem((2, frames, rows, chans), BF16), vmem((4, n_tm, 8, chans), F32)],
            [vmem((2, frames, cols, chans), BF16), vmem((4, n_tm, 8, chans), F32)],
            vmem((frames, cols * rows, chans), F32),
            vmem((frames + 2, cols * rows, chans), BF16),
            vmem((cols, frames, rows, chans), BF16),
            vmem((pair, cols * rows, chans), F32),
            vmem((pair, cols + 2, rows, 3 * chans), BF16),
            vmem((chans, offs * offs * chans), F32),
            vmem((chans, lags * chans), F32),
            sum_bufs(s_taps),
            sum_bufs(t_taps),
            vmem((n_w * s_taps, chans, chans), BF16),
            vmem((n_w * t_taps, chans, chans), BF16),
            vmem((lags * chans, chans), BF16),
            vmem((lags * chans, chans), BF16),
            vmem((offs * offs * chans, chans), BF16),
            vmem((offs * offs * chans, chans), BF16),
            pltpu.SMEM(lengths.shape, jnp.int32),
            vmem(temporal_weight.shape, BF16),
            vmem(spatial_weight.shape, BF16),
            dma((5 + chunks,)), dma((n_tm,)), dma((n_tm,)), dma((2, n_h)), dma((2, n_h)), dma((2, 8)), dma((2, 8)),
            dma((n_tm, 8)), dma((n_tm, 8)), dma((chunks, n_h)), dma((chunks, n_h)),
            sum_sems(),
            sum_sems(),
        ],
        compiler_params=pltpu.CompilerParams(collective_id=0, has_side_effects=True, vmem_limit_bytes=54 << 20),
    )(video, out_grad, lengths, temporal_weight, spatial_weight)
    return (
        video_grad,
        t_sum.astype(F32),
        s_sum.astype(F32).reshape(offs, offs, chans, chans),
    )


def solution(mesh):
    placed = (
        P("width", ("tm", "height"), None, None, None),
        P("width", None, "tm", "height", None),
        P(),
        P(),
        P(),
    )
    return jax.shard_map(
        functools.partial(shards, mesh.shape["tm"], mesh.shape["height"], mesh.shape["width"]),
        mesh=mesh,
        in_specs=placed,
        out_specs=(P("width", ("tm", "height"), None, None, None), P(), P()),
        check_vma=False,
    )
```

```python
import functools

import jax
import jax.numpy as jnp
from jax import lax
from jax.experimental import pallas as pl
from jax.experimental.pallas import tpu as pltpu
from jax.sharding import PartitionSpec as P

MESH = pl.DeviceIdType.MESH
BF16 = jnp.bfloat16
F32 = jnp.float32


def started(copy):
    def body(d, carry):
        copy(d).start()
        return carry

    return body


def waited(copy):
    def body(d, carry):
        copy(d).wait()
        return carry

    return body


def kernel(
    n_tm, n_h, n_w, scale,
    video, out_grad, lengths_in, t_weight_in, s_weight_in,
    video_grad, t_sum, s_sum,
    clip, grads, act, act_side, act_got, act_sent, delta, delta_got, delta_sent,
    slope, act_grad, moved, plane, wide, s_total, t_total, s_bufs, t_bufs, s_out, t_out,
    t_fwd, t_bwd, s_fwd, s_bwd, lengths, t_weight, s_weight,
    local_sem, vz_send, vz_recv, vh_send, vh_recv, a_send, a_recv, d_send, d_recv, o_send, o_recv, s_sems, t_sems,
):
    tm = lax.axis_index("tm")
    h = lax.axis_index("height")
    w = lax.axis_index("width")
    frames, cols, rows, chans = delta.shape
    pair = frames // n_tm
    up, down = (h + n_h - 1) % n_h, (h + 1) % n_h
    block = w * n_tm + tm
    blocks = n_w * n_tm
    left, right = (block + blocks - 1) % blocks, (block + 1) % blocks
    left_tm, left_w = left % n_tm, left // n_tm
    right_tm, right_w = right % n_tm, right // n_tm
    around = (
        (tm, up, w), (tm, down, w), (left_tm, h, left_w), (right_tm, h, right_w),
        (left_tm, up, left_w), (left_tm, down, left_w), (right_tm, up, right_w), (right_tm, down, right_w),
    )

    loads = [
        pltpu.make_async_copy(src, dst, local_sem.at[i])
        for i, (src, dst) in enumerate(((t_weight_in, t_weight), (s_weight_in, s_weight), (lengths_in, lengths)))
    ]
    for load in loads:
        load.start()
    barrier = pltpu.get_barrier_semaphore()

    def greet_h(d, carry):
        pl.semaphore_signal(barrier, inc=1, device_id=(tm, (h + d) % n_h, w), device_id_type=MESH)
        return carry

    def greet_z(d, carry):
        pl.semaphore_signal(barrier, inc=1, device_id=((tm + d) % n_tm, h, w), device_id_type=MESH)
        return carry

    lax.fori_loop(1, n_tm, greet_z, 0)
    lax.fori_loop(1, n_h, greet_h, 0)
    pl.semaphore_signal(barrier, inc=1, device_id=(tm, h, 1 - w), device_id_type=MESH)
    for other in around[2:]:
        pl.semaphore_signal(barrier, inc=1, device_id=other, device_id_type=MESH)
    pl.semaphore_wait(barrier, n_tm - 1 + n_h - 1 + 1 + 6)

    def vz_copy(d):
        to = (tm + d) % n_tm
        return pltpu.make_async_remote_copy(
            src_ref=out_grad.at[0, pl.ds(to * cols, cols)], dst_ref=grads.at[tm],
            send_sem=vz_send.at[d], recv_sem=vz_recv.at[d], device_id=(to, h, w), device_id_type=MESH)

    parts_in = vh_send.shape[0]
    run = frames // parts_in

    def vh_copy(i):
        def copy(d):
            to = (h + d) % n_h
            return pltpu.make_async_remote_copy(
                src_ref=video.at[0, 0, pl.ds(i * run, run), pl.ds(pl.multiple_of(to * rows, rows), rows)],
                dst_ref=clip.at[h, pl.ds(2 + i * run, run)],
                send_sem=vh_send.at[i, d], recv_sem=vh_recv.at[i, d], device_id=(tm, to, w), device_id_type=MESH)

        return copy

    def step_of(j):
        return (((j + 1) // 2) * (2 * (j % 2) - 1) + n_tm) % n_tm

    for i in range(parts_in):
        lax.fori_loop(1, n_h, started(vh_copy(i)), 0)
    lax.fori_loop(1, n_tm, lambda j, carry: started(vz_copy)(step_of(j), carry), 0)
    own_grad = pltpu.make_async_copy(out_grad.at[0, pl.ds(tm * cols, cols)], grads.at[tm], local_sem.at[3])
    own_clip = pltpu.make_async_copy(
        video.at[0, 0, :, pl.ds(pl.multiple_of(h * rows, rows), rows)], clip.at[h, pl.ds(2, frames)], local_sem.at[4])
    own_grad.start()
    own_clip.start()

    for f in range(2):
        clip[:, f] = jnp.zeros((cols, rows, chans), BF16)
        act_grad[frames + f] = jnp.zeros((cols * rows, chans), BF16)
    for load in loads:
        load.wait()
    for k in range(3):
        t_fwd[k * chans : (k + 1) * chans, :] = t_weight[k]
        t_bwd[k * chans : (k + 1) * chans, :] = t_weight[k].T
    for b in range(3):
        for a in range(3):
            place = pl.ds((b * 3 + a) * chans, chans)
            s_fwd[place, :] = s_weight[a, b]
            s_bwd[place, :] = s_weight[a, b].T
    s_total[...] = jnp.zeros_like(s_total)
    t_total[...] = jnp.zeros_like(t_total)
    delta_sent[1][...] = jnp.zeros_like(delta_sent[1])
    starts = [lengths[0], lengths[0] + lengths[1], lengths[0] + lengths[1] + lengths[2]]

    def mask(f, lag):
        keep = jnp.where(f >= lag, 1, 0)
        for start in starts:
            keep = jnp.where((start > f - lag) & (start <= f), 0, keep)
        return jnp.broadcast_to(keep.astype(F32), (rows, chans)).astype(BF16)[None]

    own_clip.wait()

    def edges_of(value, sent, corner_at, f, i):
        edge, corner = sent
        plane[i] = value.astype(F32)
        edge[0, f] = plane[i, pl.ds(0, cols, stride=rows), :].astype(BF16)
        edge[1, f] = plane[i, pl.ds(rows - 1, cols, stride=rows), :].astype(BF16)
        for k, place in enumerate((0, rows - 1, (cols - 1) * rows, cols * rows - 1)):
            corner[corner_at(k)] = plane[i, place : place + 1, :]

    def act_corner(f):
        return lambda k: (k, pl.ds(f, 1))

    def delta_corner(t, i):
        return lambda k: (k, t, pl.ds(i, 1))

    def flat(blocks):
        return [block.reshape(cols * rows, chans) for block in blocks]

    def act_pair(t, carry):
        lines = []
        for i in range(pair):
            f = t * pair + i
            lines.append(jnp.concatenate(flat([clip[:, f + 2], clip[:, f + 1] * mask(f, 1), clip[:, f] * mask(f, 2)]), axis=1))
        both = jnp.dot(jnp.concatenate(lines, axis=0), t_fwd[...], preferred_element_type=F32).astype(BF16)
        for i in range(pair):
            value = both[i * cols * rows : (i + 1) * cols * rows]
            act[t * pair + i, 1 : cols + 1, :, chans : 2 * chans] = value.reshape(cols, rows, chans)
            act_side[0, t * pair + i] = value[:rows]
            act_side[1, t * pair + i] = value[(cols - 1) * rows :]
            edges_of(value, act_sent, act_corner(t * pair + i), t * pair + i, i)
        return carry

    def halo_copies(sent, got, first, last, span, part, send, recv):
        (edge, corner), (got_rows, got_cols, got_corner) = sent, got
        parts = [
            (edge.at[0, span], got_rows.at[1, span]), (edge.at[1, span], got_rows.at[0, span]),
            (first, got_cols.at[1, span]), (last, got_cols.at[0, span]),
        ] + [(corner.at[(k, *part)], got_corner.at[(3 - k, *part)]) for k in range(4)]
        return [
            pltpu.make_async_remote_copy(
                src_ref=src, dst_ref=dst, send_sem=send.at[i], recv_sem=recv.at[i], device_id=around[i], device_id_type=MESH)
            for i, (src, dst) in enumerate(parts)
        ]

    def act_halo(i):
        span = pl.ds(i * run, run)
        return halo_copies(
            act_sent, act_got, act_side.at[0, span], act_side.at[1, span], span, (span,), a_send.at[i], a_recv.at[i])

    for i in range(parts_in):
        lax.fori_loop(1, n_h, waited(vh_copy(i)), 0)
        lax.fori_loop(i * run // pair, (i + 1) * run // pair, act_pair, 0)
        for copy in act_halo(i):
            copy.start()

    row = lax.broadcasted_iota(jnp.int32, (rows, chans), 0)
    is_first, is_last = row == 0, row == rows - 1
    has_up, has_down = h > 0, h < n_h - 1
    has_side = (block > 0, block < blocks - 1)

    def kept(flag, value):
        return jnp.where(flag, value, jnp.zeros_like(value))

    def shifted(middle, above, below):
        before = jnp.where(is_first, jnp.broadcast_to(above, middle.shape), pltpu.roll(middle, 1, 0))
        after = jnp.where(is_last, jnp.broadcast_to(below, middle.shape), pltpu.roll(middle, rows - 1, 0))
        return before.astype(BF16), after.astype(BF16)

    def with_halo(f, middle_of, got, corner_at, put):
        got_rows, got_cols, got_corner = got
        above = kept(has_up, got_rows[0, f].astype(F32))
        below = kept(has_down, got_rows[1, f].astype(F32))
        for c in range(cols):
            middle = middle_of(c)
            before, after = shifted(middle.astype(F32), above[c : c + 1], below[c : c + 1])
            put(c + 1, before, middle, after)
        for side, c in ((0, 0), (1, cols + 1)):
            middle = kept(has_side[side], got_cols[side, f].astype(F32))
            above_side = kept(has_side[side] & has_up, got_corner[corner_at(2 * side)])
            below_side = kept(has_side[side] & has_down, got_corner[corner_at(2 * side + 1)])
            before, after = shifted(middle, above_side, below_side)
            put(c, before, middle.astype(BF16), after)


    def slope_pair(t, carry):
        lines = []
        for i in range(pair):
            f = t * pair + i

            def put(c, before, middle, after):
                act[f, c, :, 0:chans] = before
                if c == 0 or c == cols + 1:
                    act[f, c, :, chans : 2 * chans] = middle
                act[f, c, :, 2 * chans : 3 * chans] = after

            with_halo(f, lambda c: act[f, c + 1, :, chans : 2 * chans], act_got, act_corner(f), put)
            lines.append(
                jnp.concatenate([act[f, b : b + cols].reshape(cols * rows, 3 * chans) for b in range(3)], axis=1))
        pre = jnp.dot(jnp.concatenate(lines, axis=0), s_fwd[...], preferred_element_type=F32)
        sig = jax.nn.sigmoid(pre)
        slope[pl.ds(t * pair, pair)] = (sig * (1.0 + pre * (1.0 - sig))).reshape(pair, cols * rows, chans)
        return carry

    for i in range(parts_in):
        for copy in act_halo(i):
            copy.wait()
        lax.fori_loop(i * run // pair, (i + 1) * run // pair, slope_pair, 0)

    def delta_halo(t):
        span = pl.ds(t * pair, pair)
        return halo_copies(
            delta_sent, delta_got, delta.at[span, 0], delta.at[span, cols - 1], span, (t,), d_send.at[t], d_recv.at[t])

    own_grad.wait()

    def delta_pair(j, carry):
        d = step_of(j)
        t = (tm + n_tm - d) % n_tm

        @pl.when(j > 0)
        def _():
            vz_copy(d).wait()

        for i in range(pair):
            f = t * pair + i
            value = (grads[t, :, i].reshape(cols * rows, chans).astype(F32) * slope[f]).astype(BF16)
            delta[f] = value.reshape(cols, rows, chans)
            edges_of(value, delta_sent, delta_corner(t, i), f, i)
        for copy in delta_halo(t):
            copy.start()
        return carry

    def spatial_part(t, carry):
        span = pl.ds(t * 2 * pair, 2 * pair)
        here = delta[span].reshape(2 * pair * cols * rows, chans)
        for b in range(3):
            source = act[span, b : b + cols].reshape(2 * pair * cols * rows, 3 * chans)
            s_total[:, b * 3 * chans : (b + 1) * 3 * chans] += lax.dot_general(
                here, source, (((0,), (0,)), ((), ())), preferred_element_type=F32)
        return carry

    def back_pair(t):
        for copy in delta_halo(t):
            copy.wait()
        lines = []
        for i in range(pair):
            f = t * pair + i

            def put(c, before, middle, after):
                wide[i, c, :, 0:chans] = after
                wide[i, c, :, chans : 2 * chans] = middle
                wide[i, c, :, 2 * chans : 3 * chans] = before

            with_halo(f, lambda c: delta[f, c], delta_got, delta_corner(t, i), put)
            lines.append(jnp.concatenate(
                [wide[i, 2 - b : 2 - b + cols].reshape(cols * rows, 3 * chans) for b in range(3)], axis=1))
        value = jnp.dot(jnp.concatenate(lines, axis=0), s_bwd[...], preferred_element_type=F32).astype(BF16)
        act_grad[pl.ds(t * pair, pair)] = value.reshape(pair, cols * rows, chans)

    lax.fori_loop(0, n_tm, delta_pair, 0)
    lax.fori_loop(0, n_tm // 2, spatial_part, 0)

    def device(t, row_band, core):
        return {"device_id": (t, row_band, core), "device_id_type": MESH}

    def summed_over_all(terms, out, bufs, sems):
        pair_buf, half, h_buf, z_buf, got_mine, got_theirs = bufs
        swap_sem, h_send, h_recv, z_send, z_recv, g_send, g_recv, f_sem = sems
        taps = half.shape[0]
        piece = chans // n_h
        mine, theirs = pl.ds(w * taps, taps), pl.ds((1 - w) * taps, taps)

        def band(i):
            return pl.ds(pl.multiple_of(i * piece, piece), piece)

        swap = pltpu.make_async_remote_copy(
            src_ref=terms.at[theirs], dst_ref=pair_buf, send_sem=swap_sem.at[0], recv_sem=swap_sem.at[1],
            **device(tm, h, 1 - w))

        def h_copy(d):
            to = (h + d) % n_h
            return pltpu.make_async_remote_copy(
                src_ref=half.at[:, band(to)], dst_ref=h_buf.at[d], send_sem=h_send.at[d], recv_sem=h_recv.at[d],
                **device(tm, to, w))

        def z_copy(d):
            return pltpu.make_async_remote_copy(
                src_ref=z_buf.at[tm], dst_ref=z_buf.at[tm], send_sem=z_send.at[d], recv_sem=z_recv.at[d],
                **device((tm + d) % n_tm, h, w))

        def g_copy(d):
            return pltpu.make_async_remote_copy(
                src_ref=got_mine.at[h], dst_ref=got_mine.at[h], send_sem=g_send.at[d], recv_sem=g_recv.at[d],
                **device(tm, (h + d) % n_h, w))

        share = pltpu.make_async_remote_copy(
            src_ref=got_mine, dst_ref=got_theirs, send_sem=f_sem.at[0], recv_sem=f_sem.at[1],
            **device(tm, h, 1 - w))

        def gather(place, got):
            for i in range(0, n_h, 2):
                both = jnp.concatenate([got[i].astype(F32), got[i + 1].astype(F32)], axis=1)
                out[place, i * piece : (i + 2) * piece, :] = both.astype(BF16)

        def stage0():
            swap.start()

        def stage1():
            swap.wait()
            half[...] = terms[mine] + pair_buf[...]
            lax.fori_loop(1, n_h, started(h_copy), 0)

        def stage2():
            lax.fori_loop(1, n_h, waited(h_copy), 0)
            total = half[:, band(h), :]
            for d in range(1, n_h):
                total = total + h_buf[d]
            z_buf[tm] = total
            lax.fori_loop(1, n_tm, started(z_copy), 0)

        def stage3():
            lax.fori_loop(1, n_tm, waited(z_copy), 0)
            total = z_buf[0]
            for t in range(1, n_tm):
                total = total + z_buf[t]
            got_mine[h] = total.astype(BF16)
            lax.fori_loop(1, n_h, started(g_copy), 0)

        def stage4():
            lax.fori_loop(1, n_h, waited(g_copy), 0)
            share.start()
            gather(mine, got_mine)

        def stage5():
            share.wait()
            gather(theirs, got_theirs)

        return stage0, stage1, stage2, stage3, stage4, stage5

    s_terms, t_terms = s_bufs[0], t_bufs[0]
    s_stage = summed_over_all(s_terms, s_out, s_bufs[1:], s_sems)
    t_stage = summed_over_all(t_terms, t_out, t_bufs[1:], t_sems)
    for a in range(3):
        for b in range(3):
            s_terms[a * 3 + b] = s_total[:, (b * 3 + a) * chans : (b * 3 + a + 1) * chans].T * scale
    for k in range(9, s_terms.shape[0]):
        s_terms[k] = jnp.zeros((chans, chans), F32)
    s_stage[0]()

    def parts_of(t):
        lines = []
        for i in range(pair):
            f = t * pair + i
            lines.append(jnp.concatenate([
                act_grad[f],
                (act_grad[f + 1].reshape(cols, rows, chans) * mask(f + 1, 1)).reshape(cols * rows, chans),
                (act_grad[f + 2].reshape(cols, rows, chans) * mask(f + 2, 2)).reshape(cols * rows, chans),
            ], axis=1))
        return lines

    def weight_pair(t):
        here = jnp.concatenate(flat([clip[:, t * pair + 2 + i] for i in range(pair)]), axis=0)
        parts = jnp.concatenate(parts_of(t), axis=0)
        t_total[...] += lax.dot_general(here, parts, (((0,), (0,)), ((), ())), preferred_element_type=F32)
        return parts

    def video_pair(t, parts):
        value = jnp.dot(parts, t_bwd[...], preferred_element_type=F32).astype(BF16)
        for i in range(pair):
            moved[:, t * pair + i] = value[i * cols * rows : (i + 1) * cols * rows].reshape(cols, rows, chans)

    def back_time(t, carry):
        back_pair(t)

        @pl.when(t >= 1)
        def _():
            video_pair(t - 1, weight_pair(t - 1))

        return carry

    chunks = o_send.shape[0]
    length = frames // chunks

    def out_place(i):
        return video_grad.at[0, 0, pl.ds(i * length, length), pl.ds(pl.multiple_of(h * rows, rows), rows)]

    def out_copy(i):
        def copy(d):
            to = (h + d) % n_h
            return pltpu.make_async_remote_copy(
                src_ref=moved.at[to, pl.ds(i * length, length)], dst_ref=out_place(i),
                send_sem=o_send.at[i, d], recv_sem=o_recv.at[i, d], **device(tm, to, w))

        return copy

    def own_out(i):
        return pltpu.make_async_copy(moved.at[h, pl.ds(i * length, length)], out_place(i), local_sem.at[5 + i])

    def send_back(i):
        lax.fori_loop(1, n_h, started(out_copy(i)), 0)
        own_out(i).start()

    after = {0: s_stage[1], 2: s_stage[2]}
    per = n_tm // chunks
    for i in range(chunks):
        lax.fori_loop(i * per + (i > 0), min((i + 1) * per + 1, n_tm), back_time, 0)
        if i in after:
            after[i]()
        if i < chunks - 1:
            send_back(i)
    last_parts = weight_pair(n_tm - 1)
    for k in range(3):
        t_terms[k] = t_total[:, k * chans : (k + 1) * chans] * scale
    for k in range(3, t_terms.shape[0]):
        t_terms[k] = jnp.zeros((chans, chans), F32)
    t_stage[0]()
    video_pair(n_tm - 1, last_parts)
    t_stage[1]()
    t_stage[2]()
    send_back(chunks - 1)
    s_stage[3]()
    t_stage[3]()
    s_stage[4]()
    t_stage[4]()
    s_stage[5]()
    s_sum[...] = s_out[0 : s_sum.shape[0]]
    for i in range(chunks):
        own_out(i).wait()
        lax.fori_loop(1, n_h, waited(out_copy(i)), 0)
    t_stage[5]()
    t_sum[...] = t_out[0 : t_sum.shape[0]]


def shards(n_tm, n_h, n_w, video, out_grad, lengths, temporal_weight, spatial_weight):
    frames, all_rows, chans = video.shape[2:]
    rows = all_rows // n_h
    cols = out_grad.shape[1] // n_tm
    pair = frames // n_tm
    lags = temporal_weight.shape[0]
    offs = spatial_weight.shape[0]
    s_taps = -(-offs * offs // n_w)
    t_taps = -(-lags // n_w)
    chunks = 4
    scale = float(frames * all_rows * cols * n_tm * n_w) ** (-0.5)
    dma = pltpu.SemaphoreType.DMA
    vmem = pltpu.VMEM

    def sum_bufs(taps):
        return [
            vmem((n_w * taps, chans, chans), F32),
            vmem((taps, chans, chans), F32),
            vmem((taps, chans, chans), F32),
            vmem((n_h, taps, chans // n_h, chans), F32),
            vmem((n_tm, taps, chans // n_h, chans), F32),
            vmem((n_h, taps, chans // n_h, chans), BF16),
            vmem((n_h, taps, chans // n_h, chans), BF16),
        ]

    def sum_sems():
        return [dma((2,)), dma((n_h,)), dma((n_h,)), dma((n_tm,)), dma((n_tm,)), dma((n_h,)), dma((n_h,)), dma((2,))]

    hbm = pl.BlockSpec(memory_space=pltpu.HBM)
    video_grad, t_sum, s_sum = pl.pallas_call(
        functools.partial(kernel, n_tm, n_h, n_w, scale),
        out_shape=(
            jax.ShapeDtypeStruct(video.shape, BF16),
            jax.ShapeDtypeStruct((lags, chans, chans), BF16),
            jax.ShapeDtypeStruct((offs * offs, chans, chans), BF16),
        ),
        in_specs=[hbm] * 5,
        out_specs=(
            pl.BlockSpec(memory_space=pl.ANY), pl.BlockSpec(memory_space=pltpu.VMEM), pl.BlockSpec(memory_space=pltpu.VMEM)),
        scratch_shapes=[
            vmem((cols, frames + 2, rows, chans), BF16),
            vmem((n_tm, cols, pair, rows, chans), BF16),
            vmem((frames, cols + 2, rows, 3 * chans), BF16),
            vmem((2, frames, rows, chans), BF16),
            [vmem((2, frames, cols, chans), BF16), vmem((2, frames, rows, chans), BF16), vmem((4, frames, chans), F32)],
            [vmem((2, frames, cols, chans), BF16), vmem((4, frames, chans), F32)],
            vmem((frames, cols, rows, chans), BF16),
            [vmem((2, frames, cols, chans), BF16), vmem((2, frames, rows, chans), BF16), vmem((4, n_tm, 8, chans), F32)],
            [vmem((2, frames, cols, chans), BF16), vmem((4, n_tm, 8, chans), F32)],
            vmem((frames, cols * rows, chans), F32),
            vmem((frames + 2, cols * rows, chans), BF16),
            vmem((cols, frames, rows, chans), BF16),
            vmem((pair, cols * rows, chans), F32),
            vmem((pair, cols + 2, rows, 3 * chans), BF16),
            vmem((chans, offs * offs * chans), F32),
            vmem((chans, lags * chans), F32),
            sum_bufs(s_taps),
            sum_bufs(t_taps),
            vmem((n_w * s_taps, chans, chans), BF16),
            vmem((n_w * t_taps, chans, chans), BF16),
            vmem((lags * chans, chans), BF16),
            vmem((lags * chans, chans), BF16),
            vmem((offs * offs * chans, chans), BF16),
            vmem((offs * offs * chans, chans), BF16),
            pltpu.SMEM(lengths.shape, jnp.int32),
            vmem(temporal_weight.shape, BF16),
            vmem(spatial_weight.shape, BF16),
            dma((5 + chunks,)), dma((n_tm,)), dma((n_tm,)), dma((2, n_h)), dma((2, n_h)), dma((2, 8)), dma((2, 8)),
            dma((n_tm, 8)), dma((n_tm, 8)), dma((chunks, n_h)), dma((chunks, n_h)),
            sum_sems(),
            sum_sems(),
        ],
        compiler_params=pltpu.CompilerParams(collective_id=0, has_side_effects=True, vmem_limit_bytes=54528 << 10),
    )(video, out_grad, lengths, temporal_weight, spatial_weight)
    return (
        video_grad,
        t_sum.astype(F32),
        s_sum.astype(F32).reshape(offs, offs, chans, chans),
    )


def solution(mesh):
    placed = (
        P("width", ("tm", "height"), None, None, None),
        P("width", None, "tm", "height", None),
        P(),
        P(),
        P(),
    )
    return jax.shard_map(
        functools.partial(shards, mesh.shape["tm"], mesh.shape["height"], mesh.shape["width"]),
        mesh=mesh,
        in_specs=placed,
        out_specs=(P("width", ("tm", "height"), None, None, None), P(), P()),
        check_vma=False,
    )
```
